32 devices in a mesh: outer: 8 (over y, x, core), inner: 4 (over z).
Axes of the slice: x: 2, y: 2, z: 4, core: 2. Of those that a mesh axis runs over, the one named last changes fastest.
Arguments:
- output_grad: bfloat16 [8192, 1024], P(('outer', 'inner')), may hold values from -3 to 3
- expert_ids: int32 [8192, 2], P(('outer', 'inner')), may hold values from 0 to 31, all different within a row; in each aligned block of 256 rows (0 to 255, 256 to 511, ...) at most 24 rows name the same one
- gate_weights: float32 [8192, 2], P(('outer', 'inner')), may hold values from 0.2 to 1
- pre_act: bfloat16 [32, 768, 4096], P(('outer', 'inner')), may hold values from -6 to 6
- w_in: bfloat16 [32, 1024, 4096], P(('outer', 'inner')), may hold values from -0.1875 to 0.1875
- w_out: bfloat16 [32, 4096, 1024], P(('outer', 'inner')), may hold values from -0.09375 to 0.09375
Outputs:
- input_grad: bfloat16 [8192, 1024], P(('outer', 'inner'))
- gate_grad: float32 [8192, 2], P(('outer', 'inner'))
The draws below stay inside these ranges and needn't reach their ends.
Inputs may be any that keep to these rules, and one draw needn't show every extreme that they name: `expert_ids`: the two experts of a token differ. Among the 256 tokens of one device no expert is named more than 24 times, a bound that some block reaches.
All inputs are finite; a program needn't handle non-finite values.
Results may differ from the reference program's by a relative error of at most 0.013.
Values may be sent and summed in bfloat16 or wider, within the bound.
No kernel may reach another device: no remote copies, remote signals or barrier semaphores. Data moves between devices by JAX's collectives and lax.ppermute only.
A program may use at most 128 MiB of HBM per device.

```python
import math
import jax
import jax.numpy as jnp
import numpy as np
from jax import lax

D = 1024
FF = 4096
TOK_DEV = 256
EXPERTS = 32
TOKENS = 8192
MOST = 24
CAP = 768


def steps_of(rng, dims, pieces, low, high):
    factor_of = 1.0
    for axis_at, shards_of in pieces:
        heights = jax.random.uniform(jax.random.fold_in(jax.random.fold_in(rng, 6), axis_at), (shards_of,), jnp.float32, low / len(pieces), high / len(pieces))
        factor_of = factor_of * jnp.repeat(jnp.exp(heights), dims[axis_at] // shards_of).reshape((-1,) + (1,) * (len(dims) - 1 - axis_at))
    return factor_of


def routed_block(rng, own, number, rows, amount, top, limit, lean):
    sequence = jax.random.permutation(rng, amount)
    heavy_load, common = shares(amount, rows * top, limit, lean, True), shares(amount, rows * top, limit, lean, False)
    places = jnp.arange(amount)

    def named(tallies, rotation):
        used = int((tallies > 0).sum())
        fixed = max(1, used // 4)
        moved = fixed + (places - fixed + rotation * (used - fixed)) % max(1, amount - fixed)
        return jnp.zeros((amount,), jnp.int32).at[sequence[jnp.where(places < fixed, places, moved)]].set(jnp.asarray(tallies, jnp.int32))

    tallies = jnp.where(number % 4 == 0, named(heavy_load, number // 4), named(common, number - number // 4 - 1))
    mixed = jax.random.permutation(jax.random.fold_in(own, 3), amount)
    giver, sink = mixed[0:amount // 2 * 2:2], mixed[1:amount // 2 * 2:2]
    room = jnp.minimum(tallies[giver] - 1, limit - tallies[sink]) // 2
    room = jnp.where((giver == sequence[0]) | (sink == sequence[0]) | (tallies[sink] == 0), 0, jnp.maximum(room, 0))
    moved = jax.random.randint(jax.random.fold_in(own, 4), (amount // 2,), 0, 1 << 20) % (room + 1)
    tallies = tallies.at[giver].add(-moved).at[sink].add(moved)
    members = jnp.searchsorted(jnp.cumsum(tallies), jnp.arange(rows * top), side="right").astype(jnp.int32)
    listing = members.reshape(top, rows).T
    listing = listing[jax.random.permutation(jax.random.fold_in(own, 1), rows)]
    rotation = jax.random.randint(jax.random.fold_in(own, 2), (rows, 1), 0, top)
    return jnp.take_along_axis(listing, (jnp.arange(top)[None, :] + rotation) % top, axis=1)


def shares(amount, total, bound, skew, full):
    weights = [(1 << 20) // math.isqrt(standing ** skew) + 1 for standing in range(1, amount + 1)]
    largest = bound if full else min(bound, max(-(-total // amount), total * weights[0] // sum(weights)))
    least = 1 if total - largest >= amount - 1 else 0
    holding, surplus = [largest] + [least] * (amount - 1), total - largest - least * (amount - 1)
    while surplus > 0:
        free = [i for i in range(1, amount) if holding[i] < largest] or [i for i in range(1, amount) if holding[i] < bound]
        mass, remaining = sum([weights[i] for i in free]), surplus
        for i in free:
            more = min(bound - holding[i], max(1, remaining * weights[i] // mass), surplus)
            holding[i] = holding[i] + more
            surplus = surplus - more
    return np.array(holding)


def noise(key, dims, deviation, most, split=(), kind=jnp.bfloat16):
    gain = steps_of(key, dims, split, -0.22, 0.18) if split else 1.0
    drawn = jax.random.normal(key, dims, jnp.float32) * deviation * gain
    return jnp.minimum(jnp.maximum(drawn, -most), most).astype(kind)


def setup_inputs(seed: int = 0) -> dict:
    seeds = jax.random.split(jax.random.key(seed), 7)
    output_grad = noise(seeds[0], (TOKENS, D), 0.5, 3.0, ((0, 32),))
    expert_ids_keys = jax.random.split(jax.random.fold_in(seeds[1], 1), TOKENS // TOK_DEV)
    expert_ids_turns = jax.random.permutation(jax.random.fold_in(seeds[1], 3), TOKENS // TOK_DEV)
    expert_ids = jax.vmap(lambda own, number: routed_block(jax.random.fold_in(seeds[1], 2), own, number, TOK_DEV, EXPERTS, 2, MOST, 2))(expert_ids_keys, expert_ids_turns).reshape((TOKENS, 2))
    gate_weights = jnp.clip(0.2 + 0.8 * jax.random.uniform(seeds[2], (TOKENS, 2), jnp.float32) ** steps_of(seeds[2], (TOKENS, 2), ((0, 32),), -0.2, 0.2), 0.2, 1.0)
    pre_act = noise(seeds[3], (EXPERTS, CAP, FF), 1.0, 6.0, ((0, 32),))
    w_in = noise(seeds[4], (EXPERTS, D, FF), D ** -0.5, 0.1875, ((0, 32),))
    w_out = noise(seeds[5], (EXPERTS, FF, D), FF ** -0.5, 0.09375, ((0, 32),))
    return dict(output_grad=output_grad, expert_ids=expert_ids, gate_weights=gate_weights, pre_act=pre_act, w_in=w_in, w_out=w_out)


def expert_part(operands):
    slot_rows, gate_col, pre_rows, w_in_e, w_out_e = operands
    upstream = jnp.dot(slot_rows, w_out_e.T, preferred_element_type=jnp.float32)
    relu_out = jnp.maximum(pre_rows.astype(jnp.float32), 0.0)
    slot_gate = jnp.sum(relu_out * upstream, axis=1)
    hidden_grad = jnp.where(pre_rows > 0, gate_col[:, None] * upstream, 0.0).astype(jnp.bfloat16)
    row_grad = jnp.dot(hidden_grad, w_in_e.T, preferred_element_type=jnp.float32).astype(jnp.bfloat16)
    return row_grad, slot_gate


def reference(output_grad, expert_ids, gate_weights, pre_act, w_in, w_out):
    devices = TOKENS // TOK_DEV
    flat_ids = expert_ids.reshape(-1).astype(jnp.int32)
    entries = flat_ids.shape[0]
    onehot = (flat_ids[:, None] == jnp.arange(EXPERTS, dtype=jnp.int32)[None, :]).astype(jnp.int32)
    onehot = onehot.reshape(devices, 2 * TOK_DEV, EXPERTS)
    earlier = (jnp.cumsum(onehot, axis=1) - onehot).astype(jnp.int32)
    slot_pos = jnp.sum(earlier * onehot, axis=2).reshape(-1).astype(jnp.int32)
    source = (jnp.arange(entries, dtype=jnp.int32) // (2 * TOK_DEV)).astype(jnp.int32)
    cap_row = (source * MOST + slot_pos).astype(jnp.int32)
    token_of = (jnp.arange(entries, dtype=jnp.int32) // 2).astype(jnp.int32)
    dispatched = jnp.zeros((EXPERTS, CAP, D), jnp.bfloat16).at[flat_ids, cap_row].set(output_grad[token_of])
    gate_buf = jnp.zeros((EXPERTS, CAP), jnp.float32).at[flat_ids, cap_row].set(gate_weights.reshape(-1).astype(jnp.float32))
    row_grad, slot_gate = lax.map(expert_part, (dispatched, gate_buf, pre_act, w_in, w_out))
    picked = row_grad[flat_ids, cap_row].astype(jnp.float32).reshape(TOKENS, 2, D)
    input_grad = jnp.sum(picked, axis=1).astype(jnp.bfloat16)
    gate_grad = slot_gate[flat_ids, cap_row].reshape(TOKENS, 2)
    return input_grad, gate_grad
```

```python
import functools

import jax
import jax.numpy as jnp
from jax import lax
from jax.experimental import pallas as pl
from jax.experimental.pallas import tpu as pltpu
from jax.sharding import PartitionSpec as P

LANES = 128
SUBLANES = 8
NN = (((1,), (0,)), ((), ()))
NT = (((1,), (1,)), ((), ()))
TN = (((0,), (0,)), ((), ()))


def matmul(a, b, dims):
    return lax.dot_general(a, b, dims, preferred_element_type=jnp.float32)


def targets(ids, experts, per_peer):
    tokens = ids.shape[1]
    which = lax.broadcasted_iota(jnp.int32, (experts, tokens), 0)
    first, second = which == ids[0:1], which == ids[1:2]
    named = jnp.where(first | second, 1.0, 0.0).astype(jnp.bfloat16)
    before = lax.broadcasted_iota(jnp.int32, (tokens, tokens), 0) < lax.broadcasted_iota(
        jnp.int32, (tokens, tokens), 1
    )
    earlier = matmul(named, jnp.where(before, 1.0, 0.0).astype(jnp.bfloat16), NN)
    slot = [
        jnp.sum(jnp.where(mine, earlier, 0.0), axis=0, keepdims=True).astype(jnp.int32)
        for mine in (first, second)
    ]
    return ids[0:1] * per_peer + slot[0], ids[1:2] * per_peer + slot[1]


def route_body(experts, per_peer, ids_ref, tok_ref, send_ref, target_ref):
    one, two = targets(ids_ref[...], experts, per_peer)
    target_ref[0:1, :] = one
    target_ref[1:2, :] = two
    row = lax.broadcasted_iota(jnp.int32, (send_ref.shape[0], ids_ref.shape[1]), 0)
    pick = jnp.where((row == one) | (row == two), 1.0, 0.0).astype(jnp.bfloat16)
    send_ref[...] = matmul(pick, tok_ref[...], NN).astype(jnp.bfloat16)


def route(ids, tokens, experts, per_peer):
    rows, width = experts * per_peer, tokens.shape[1]
    return pl.pallas_call(
        functools.partial(route_body, experts, per_peer),
        out_shape=(
            jax.ShapeDtypeStruct((rows, width), jnp.bfloat16),
            jax.ShapeDtypeStruct(ids.shape, jnp.int32),
        ),
        cost_estimate=pl.CostEstimate(
            flops=2 * rows * tokens.shape[0] * width,
            bytes_accessed=2 * (rows + tokens.shape[0]) * width,
            transcendentals=0,
        ),
        name="route",
    )(ids, tokens)


def expert_body(blocks, packed, x_hbm, p_hbm, wo_hbm, wi_hbm, o_ref, x, p, wo, wi, acc, gsum, sem):
    rows, width = x.shape
    size = wo.shape[1]

    def up(j):
        return pltpu.make_async_copy(wo_hbm.at[pl.ds(j * size, size), :], wo.at[j], sem.at[0, j])

    def pre(j):
        return pltpu.make_async_copy(p_hbm.at[:, pl.ds(j * size, size)], p.at[j], sem.at[1, j])

    def down(j):
        return pltpu.make_async_copy(wi_hbm.at[:, pl.ds(j * size, size)], wi.at[j], sem.at[2, j])

    rows_in = pltpu.make_async_copy(x_hbm, x, sem.at[3, 0])
    rows_in.start()
    for j in range(blocks):
        up(j).start()
        pre(j).start()
        down(j).start()
    rows_in.wait()
    up(0).wait()
    upstream = matmul(x[...], wo[0], NT)
    for j in range(blocks):
        pre(j).wait()
        down(j).wait()
        following = None
        if j + 1 < blocks:
            up(j + 1).wait()
            following = matmul(x[...], wo[j + 1], NT)
        act = p[j].astype(jnp.float32)
        prod = jnp.maximum(act, 0.0) * upstream
        part = prod[:, :LANES]
        for q in range(1, size // LANES):
            part = part + prod[:, q * LANES : (q + 1) * LANES]
        hidden = jnp.where(act > 0, upstream, 0.0).astype(jnp.bfloat16)
        back = matmul(hidden, wi[j], NT)
        if j == 0:
            acc[...] = back
            gsum[...] = part
        else:
            acc[...] += back
            gsum[...] += part
        upstream = following
    dots = jnp.sum(gsum[...], axis=1, keepdims=True)
    high = dots.astype(jnp.bfloat16).astype(jnp.float32)
    low = dots - high
    out = acc[...].astype(jnp.bfloat16)
    if not packed:
        lane = lax.broadcasted_iota(jnp.int32, (rows, LANES), 1)
        o_ref[:, :width] = out
        o_ref[:, width:] = jnp.where(lane == 0, high, jnp.where(lane == 1, low, 0.0)).astype(
            jnp.bfloat16
        )
        return
    peers = o_ref.shape[0]
    groups, cols = rows // peers // SUBLANES, width // LANES
    lane = lax.broadcasted_iota(jnp.int32, (peers, SUBLANES, LANES), 2)
    out = out.reshape(peers, groups, SUBLANES, width)
    high = high.reshape(peers, groups, SUBLANES, 1)
    low = low.reshape(peers, groups, SUBLANES, 1)
    tail = jnp.zeros((peers, SUBLANES, LANES), jnp.float32)
    for r in range(groups):
        tail = jnp.where(lane == 2 * r, high[:, r], tail)
        tail = jnp.where(lane == 2 * r + 1, low[:, r], tail)
        for c in range(cols):
            at = (r * cols + c) * SUBLANES
            o_ref[:, at : at + SUBLANES, :] = out[:, r, :, c * LANES : (c + 1) * LANES]
    o_ref[:, groups * cols * SUBLANES :, :] = tail.astype(jnp.bfloat16)


def expert(x, p, wo, wi, peers, blocks):
    rows, width = x.shape
    hidden = p.shape[1]
    size = hidden // blocks
    per_peer = rows // peers
    packed = per_peer % SUBLANES == 0
    shape = (
        (peers, per_peer * (width // LANES) + SUBLANES, LANES)
        if packed
        else (rows, width + LANES)
    )
    return pl.pallas_call(
        functools.partial(expert_body, blocks, packed),
        out_shape=jax.ShapeDtypeStruct(shape, jnp.bfloat16),
        in_specs=[pl.BlockSpec(memory_space=pl.ANY)] * 4,
        out_specs=pl.BlockSpec(memory_space=pltpu.VMEM),
        scratch_shapes=[
            pltpu.VMEM((rows, width), jnp.bfloat16),
            pltpu.VMEM((blocks, rows, size), jnp.bfloat16),
            pltpu.VMEM((blocks, size, width), jnp.bfloat16),
            pltpu.VMEM((blocks, width, size), jnp.bfloat16),
            pltpu.VMEM((rows, width), jnp.float32),
            pltpu.VMEM((rows, LANES), jnp.float32),
            pltpu.SemaphoreType.DMA((4, blocks)),
        ],
        compiler_params=pltpu.CompilerParams(vmem_limit_bytes=48 << 20),
        cost_estimate=pl.CostEstimate(
            flops=4 * rows * width * hidden,
            bytes_accessed=2 * (rows * hidden + 2 * width * hidden + 2 * rows * width),
            transcendentals=0,
        ),
        name="expert",
    )(x, p, wo, wi)


def combine_body(packed, target_ref, gate_ref, back_ref, grad_ref, dots_ref):
    tokens, width = grad_ref.shape
    if packed:
        peers = back_ref.shape[0]
        cols = width // LANES
        groups = back_ref.shape[1] // SUBLANES // cols
        rows = peers * groups * SUBLANES
    else:
        rows = back_ref.shape[0]
    row = lax.broadcasted_iota(jnp.int32, (rows, tokens), 0)
    hit = [row == target_ref[k : k + 1, :] for k in range(2)]
    weight = jnp.where(
        hit[0], gate_ref[0:1, :], jnp.where(hit[1], gate_ref[1:2, :], 0.0)
    )
    high = weight.astype(jnp.bfloat16)
    low = (weight - high.astype(jnp.float32)).astype(jnp.bfloat16)
    if packed:

        def column(c):
            return jnp.stack(
                [
                    back_ref[:, (r * cols + c) * SUBLANES : (r * cols + c + 1) * SUBLANES, :]
                    for r in range(groups)
                ],
                axis=1,
            ).reshape(rows, LANES)

        tail = back_ref[:, groups * cols * SUBLANES :, :].astype(jnp.float32)
        lane = lax.broadcasted_iota(jnp.int32, tail.shape, 2)
        sums = (
            jnp.stack([jnp.where(lane // 2 == r, tail, 0.0) for r in range(groups)], axis=1)
            .reshape(rows, LANES)
            .astype(jnp.bfloat16)
        )
        for c in range(0, cols, 2):
            part = jnp.concatenate([column(c), column(c + 1)], axis=1)
            grad_ref[:, c * LANES : (c + 2) * LANES] = (
                matmul(high, part, TN) + matmul(low, part, TN)
            ).astype(jnp.bfloat16)
    else:
        part = back_ref[:, :width]
        grad_ref[...] = (matmul(high, part, TN) + matmul(low, part, TN)).astype(jnp.bfloat16)
        sums = back_ref[:, width:]
    for k in range(2):
        pick = jnp.where(hit[k], 1.0, 0.0).astype(jnp.bfloat16)
        dots_ref[k : k + 1, :] = jnp.sum(matmul(sums, pick, TN), axis=0, keepdims=True)


def combine(target, gates, back, width):
    tokens = gates.shape[1]
    packed = back.ndim == 3
    return pl.pallas_call(
        functools.partial(combine_body, packed),
        out_shape=(
            jax.ShapeDtypeStruct((tokens, width), jnp.bfloat16),
            jax.ShapeDtypeStruct(gates.shape, jnp.float32),
        ),
        compiler_params=pltpu.CompilerParams(vmem_limit_bytes=32 << 20),
        name="combine",
    )(target, gates, back)


def per_device(output_grad, expert_ids, gate_weights, pre_act, w_in, w_out):
    axes = ("outer", "inner")
    devices = lax.axis_size("outer") * lax.axis_size("inner")
    width = output_grad.shape[1]
    cap_rows = pre_act.shape[1]
    per_peer = cap_rows // devices

    def exchange(x):
        return lax.all_to_all(x, axes, split_axis=0, concat_axis=0, tiled=True)

    send, target = route(expert_ids.T, output_grad, devices, per_peer)
    received = exchange(send.reshape(devices, per_peer, width)).reshape(cap_rows, width)
    result = expert(received, pre_act[0], w_out[0], w_in[0], devices, 4)
    if result.ndim == 3:
        back = exchange(result)
    else:
        back = exchange(result.reshape(devices, per_peer, -1)).reshape(cap_rows, -1)
    input_grad, gate_grad = combine(target, gate_weights.T, back, width)
    return input_grad, gate_grad.T


def solution(mesh):
    rows = P(("outer", "inner"), None)
    blocks = P(("outer", "inner"), None, None)
    return jax.shard_map(
        per_device,
        mesh=mesh,
        in_specs=(rows, rows, rows, blocks, blocks, blocks),
        out_specs=(rows, rows),
        check_vma=False,
    )
```

```python
import functools

import jax
import jax.numpy as jnp
from jax import lax
from jax.experimental import pallas as pl
from jax.experimental.pallas import tpu as pltpu
from jax.sharding import PartitionSpec as P

LANES = 128
SUBLANES = 8
SMALL = 8 << 20
NN = (((1,), (0,)), ((), ()))
NT = (((1,), (1,)), ((), ()))
TN = (((0,), (0,)), ((), ()))


def matmul(a, b, dims):
    return lax.dot_general(a, b, dims, preferred_element_type=jnp.float32)


def slots(ids, experts):
    tokens = ids.shape[1]
    which = lax.broadcasted_iota(jnp.int32, (experts, tokens), 0)
    first, second = which == ids[0:1], which == ids[1:2]
    named = jnp.where(first | second, 1.0, 0.0).astype(jnp.bfloat16)
    before = lax.broadcasted_iota(jnp.int32, (tokens, tokens), 0) < lax.broadcasted_iota(
        jnp.int32, (tokens, tokens), 1
    )
    earlier = matmul(named, jnp.where(before, 1.0, 0.0).astype(jnp.bfloat16), NN)
    return [
        jnp.sum(jnp.where(mine, earlier, 0.0), axis=0, keepdims=True).astype(jnp.int32)
        for mine in (first, second)
    ]


def pick_rows(ids, slot, rows, per_peer, rest):
    shift = rest.bit_length() - 1
    half = lax.axis_index("half")
    row = lax.broadcasted_iota(jnp.int32, (rows, ids.shape[1]), 0)
    hits = []
    for k in range(2):
        e = ids[k : k + 1]
        peer = ((e >> (shift + 1)) << shift) | (e & (rest - 1))
        mine = ((e >> shift) & 1) == half
        hits.append(row == jnp.where(mine, peer * per_peer + slot[k], -1))
    return jnp.where(hits[0] | hits[1], 1.0, 0.0).astype(jnp.bfloat16)


def route_body(experts, per_peer, rest, ids_ref, tok_ref, send_ref, target_ref):
    ids = ids_ref[...]
    slot = slots(ids, experts)
    for k in range(2):
        target_ref[k : k + 1, :] = ids[k : k + 1] * per_peer + slot[k]
    near_pick = pick_rows(ids, slot, send_ref.shape[0], per_peer, rest)
    send_ref[...] = matmul(near_pick, tok_ref[...], NN).astype(jnp.bfloat16)


def route(ids, tokens, experts, per_peer, rest):
    rows, width = experts // 2 * per_peer, tokens.shape[1]
    return pl.pallas_call(
        functools.partial(route_body, experts, per_peer, rest),
        out_shape=(
            jax.ShapeDtypeStruct((rows, width), jnp.bfloat16),
            jax.ShapeDtypeStruct(ids.shape, jnp.int32),
        ),
        cost_estimate=pl.CostEstimate(
            flops=2 * rows * tokens.shape[0] * width,
            bytes_accessed=2 * (rows + tokens.shape[0]) * width,
            transcendentals=0,
        ),
        compiler_params=pltpu.CompilerParams(vmem_limit_bytes=60 << 20),
        name="route",
    )(ids, tokens)


def gather_body(experts, per_peer, rest, ids_ref, tok_ref, send_ref):
    ids = ids_ref[...]
    pick = pick_rows(ids, slots(ids, experts), send_ref.shape[0], per_peer, rest)
    send_ref[...] = matmul(pick, tok_ref[...], NN).astype(jnp.bfloat16)


def gather(ids, tokens, experts, per_peer, rest):
    rows, width = experts // 2 * per_peer, tokens.shape[1]
    return pl.pallas_call(
        functools.partial(gather_body, experts, per_peer, rest),
        out_shape=jax.ShapeDtypeStruct((rows, width), jnp.bfloat16),
        compiler_params=pltpu.CompilerParams(vmem_limit_bytes=SMALL),
        cost_estimate=pl.CostEstimate(flops=40 * 10**9, bytes_accessed=0, transcendentals=0),
        name="gather",
    )(ids, tokens)


def expert_body(blocks, packed, far, *refs):
    x_hbm, p_hbm, wo_hbm, wi_hbm = refs[:4]
    near_hbm = refs[4] if far else None
    o_ref, x, p, wo, wi, acc, gsum, sem = refs[4 + far :]
    rows, width = x.shape
    size = wo.shape[1]
    own = lax.axis_index("half")
    half = 1 - own if far else own

    def up(j):
        return pltpu.make_async_copy(wo_hbm.at[pl.ds(j * size, size), :], wo.at[j], sem.at[0, j])

    def pre(j):
        return pltpu.make_async_copy(
            p_hbm.at[:, half, :, pl.ds(j * size, size)], p.at[j], sem.at[1, j]
        )

    def down(j):
        return pltpu.make_async_copy(wi_hbm.at[:, pl.ds(j * size, size)], wi.at[j], sem.at[2, j])

    rows_in = pltpu.make_async_copy(x_hbm, x, sem.at[3, 0])
    rows_in.start()
    for j in range(blocks):
        up(j).start()
        pre(j).start()
        down(j).start()
    if far:
        near = pltpu.make_async_copy(near_hbm, o_ref.at[:, own], sem.at[3, 1])
        near.start()
    rows_in.wait()
    up(0).wait()
    upstream = matmul(x[...], wo[0], NT)
    for j in range(blocks):
        pre(j).wait()
        down(j).wait()
        following = None
        if j + 1 < blocks:
            up(j + 1).wait()
            following = matmul(x[...], wo[j + 1], NT)
        act = p[j].astype(jnp.float32).reshape(rows, size)
        prod = jnp.maximum(act, 0.0) * upstream
        part = prod[:, :LANES]
        for q in range(1, size // LANES):
            part = part + prod[:, q * LANES : (q + 1) * LANES]
        hidden = jnp.where(act > 0, upstream, 0.0).astype(jnp.bfloat16)
        back = matmul(hidden, wi[j], NT)
        if j == 0:
            acc[...] = back
            gsum[...] = part
        else:
            acc[...] += back
            gsum[...] += part
        upstream = following
    dots = jnp.sum(gsum[...], axis=1, keepdims=True)
    high = dots.astype(jnp.bfloat16).astype(jnp.float32)
    low = dots - high
    out = acc[...].astype(jnp.bfloat16)
    if far:
        near.wait()
    dst = o_ref.at[:, half] if far else o_ref
    if not packed:
        lane = lax.broadcasted_iota(jnp.int32, (rows, LANES), 1)
        tail = jnp.where(lane == 0, high, jnp.where(lane == 1, low, 0.0)).astype(jnp.bfloat16)
        dst[:, :, :width] = out.reshape(*dst.shape[:2], width)
        dst[:, :, width:] = tail.reshape(*dst.shape[:2], LANES)
        return
    outer, rest = dst.shape[:2]
    peers = outer * rest
    groups, cols = rows // peers // SUBLANES, width // LANES
    lane = lax.broadcasted_iota(jnp.int32, (peers, SUBLANES, LANES), 2)
    out = out.reshape(peers, groups, SUBLANES, width)
    high = high.reshape(peers, groups, SUBLANES, 1)
    low = low.reshape(peers, groups, SUBLANES, 1)
    tail = jnp.zeros((peers, SUBLANES, LANES), jnp.float32)
    for r in range(groups):
        tail = jnp.where(lane == 2 * r, high[:, r], tail)
        tail = jnp.where(lane == 2 * r + 1, low[:, r], tail)
        for c in range(cols):
            at = (r * cols + c) * SUBLANES
            dst[:, :, at : at + SUBLANES, :] = out[:, r, :, c * LANES : (c + 1) * LANES].reshape(
                outer, rest, SUBLANES, LANES
            )
    dst[:, :, groups * cols * SUBLANES :, :] = tail.astype(jnp.bfloat16).reshape(
        outer, rest, SUBLANES, LANES
    )


def expert(x, p, wo, wi, rest, blocks, near=None):
    rows, width = x.shape
    outer, _, group, hidden = p.shape
    size = hidden // blocks
    per_peer = group // rest
    far = near is not None
    packed = per_peer % SUBLANES == 0
    both = (2,) if far else ()
    shape = (
        (outer, *both, rest, per_peer * (width // LANES) + SUBLANES, LANES)
        if packed
        else (outer, *both, group, width + LANES)
    )
    operands = (x, p, wo, wi) + ((near,) if far else ())
    return pl.pallas_call(
        functools.partial(expert_body, blocks, packed, int(far)),
        out_shape=jax.ShapeDtypeStruct(shape, jnp.bfloat16),
        in_specs=[
            pl.BlockSpec(memory_space=pltpu.HBM if 1 <= i <= 3 else pl.ANY)
            for i in range(len(operands))
        ],
        out_specs=pl.BlockSpec(memory_space=pltpu.VMEM),
        scratch_shapes=[
            pltpu.VMEM((rows, width), jnp.bfloat16),
            pltpu.VMEM((blocks, outer, group, size), jnp.bfloat16),
            pltpu.VMEM((blocks, size, width), jnp.bfloat16),
            pltpu.VMEM((blocks, width, size), jnp.bfloat16),
            pltpu.VMEM((rows, width), jnp.float32),
            pltpu.VMEM((rows, LANES), jnp.float32),
            pltpu.SemaphoreType.DMA((4, blocks)),
        ],
        compiler_params=pltpu.CompilerParams(vmem_limit_bytes=50 << 20),
        cost_estimate=pl.CostEstimate(
            flops=4 * rows * width * hidden,
            bytes_accessed=2 * (rows * hidden + 2 * width * hidden + 2 * rows * width),
            transcendentals=0,
        ),
        name="expert_far" if far else "expert_near",
    )(*operands)


def combine_body(packed, target_ref, gate_ref, back_ref, grad_ref, dots_ref):
    tokens, width = grad_ref.shape
    if packed:
        peers = back_ref.shape[0]
        cols = width // LANES
        groups = back_ref.shape[1] // SUBLANES // cols
        rows = peers * groups * SUBLANES
    else:
        rows = back_ref.shape[0]
    row = lax.broadcasted_iota(jnp.int32, (rows, tokens), 0)
    hit = [row == target_ref[k : k + 1, :] for k in range(2)]
    weight = jnp.where(
        hit[0], gate_ref[0:1, :], jnp.where(hit[1], gate_ref[1:2, :], 0.0)
    )
    high = weight.astype(jnp.bfloat16)
    low = (weight - high.astype(jnp.float32)).astype(jnp.bfloat16)
    if packed:

        def column(c):
            return jnp.stack(
                [
                    back_ref[:, (r * cols + c) * SUBLANES : (r * cols + c + 1) * SUBLANES, :]
                    for r in range(groups)
                ],
                axis=1,
            ).reshape(rows, LANES)

        tail = back_ref[:, groups * cols * SUBLANES :, :].astype(jnp.float32)
        lane = lax.broadcasted_iota(jnp.int32, tail.shape, 2)
        sums = (
            jnp.stack([jnp.where(lane // 2 == r, tail, 0.0) for r in range(groups)], axis=1)
            .reshape(rows, LANES)
            .astype(jnp.bfloat16)
        )
        for c in range(0, cols, 2):
            part = jnp.concatenate([column(c), column(c + 1)], axis=1)
            grad_ref[:, c * LANES : (c + 2) * LANES] = (
                matmul(high, part, TN) + matmul(low, part, TN)
            ).astype(jnp.bfloat16)
    else:
        part = back_ref[:, :width]
        grad_ref[...] = (matmul(high, part, TN) + matmul(low, part, TN)).astype(jnp.bfloat16)
        sums = back_ref[:, width:]
    for k in range(2):
        pick = jnp.where(hit[k], 1.0, 0.0).astype(jnp.bfloat16)
        dots_ref[k : k + 1, :] = jnp.sum(matmul(sums, pick, TN), axis=0, keepdims=True)


def combine(target, gates, back, width):
    tokens = gates.shape[1]
    packed = back.ndim == 3
    return pl.pallas_call(
        functools.partial(combine_body, packed),
        out_shape=(
            jax.ShapeDtypeStruct((tokens, width), jnp.bfloat16),
            jax.ShapeDtypeStruct(gates.shape, jnp.float32),
        ),
        compiler_params=pltpu.CompilerParams(vmem_limit_bytes=16 << 20),
        name="combine",
    )(target, gates, back)


def per_device(output_grad, expert_ids, gate_weights, pre_act, w_in, w_out):
    outer, rest = lax.axis_size("outer"), lax.axis_size("rest")
    devices = 2 * outer * rest
    width = output_grad.shape[1]
    cap_rows, hidden = pre_act.shape[1:]
    per_peer = cap_rows // devices
    group = rest * per_peer
    swap = [(0, 1), (1, 0)]

    def exchange(x, axes):
        return lax.all_to_all(x, axes, split_axis=0, concat_axis=0, tiled=True)

    def to_half(rows):
        peers = rows.reshape(outer * rest, per_peer, width)
        return exchange(peers, ("outer", "rest")).reshape(outer * group, width)

    ids = expert_ids.T
    far_ids = lax.ppermute(ids, "half", swap)
    far_tokens = lax.ppermute(output_grad, "half", swap)
    send, target = route(ids, output_grad, devices, per_peer, rest)
    near_rows = to_half(send)
    far_rows = to_half(gather(far_ids, far_tokens, devices, per_peer, rest))
    act = pre_act.reshape(outer, 2, group, hidden)
    near = expert(near_rows, act, w_out[0], w_in[0], rest, 4)
    result = expert(far_rows, act, w_out[0], w_in[0], rest, 4, near)
    if result.ndim == 5:
        result = result.reshape(devices, *result.shape[3:])
    else:
        result = result.reshape(devices, per_peer, -1)
    back = exchange(result, ("outer", "half", "rest"))
    if per_peer % SUBLANES:
        back = back.reshape(cap_rows, -1)
    input_grad, gate_grad = combine(target, gate_weights.T, back, width)
    return input_grad, gate_grad.T


def solution(mesh):
    outer, inner = mesh.shape["outer"], mesh.shape["inner"]
    split = jax.sharding.Mesh(
        mesh.devices.reshape(outer, 2, inner // 2), ("outer", "half", "rest")
    )
    axes = ("outer", "half", "rest")
    rows, blocks = P(axes, None), P(axes, None, None)
    return jax.shard_map(
        per_device,
        mesh=split,
        in_specs=(rows, rows, rows, blocks, blocks, blocks),
        out_specs=(rows, rows),
        check_vma=False,
    )
```

```python
import functools

import jax
import jax.numpy as jnp
from jax import lax
from jax.experimental import pallas as pl
from jax.experimental.pallas import tpu as pltpu
from jax.sharding import PartitionSpec as P

LANES = 128
SUBLANES = 8
SMALL = 8 << 20
NN = (((1,), (0,)), ((), ()))
NT = (((1,), (1,)), ((), ()))
TN = (((0,), (0,)), ((), ()))


def matmul(a, b, dims):
    return lax.dot_general(a, b, dims, preferred_element_type=jnp.float32)


def slots(ids, experts):
    tokens = ids.shape[1]
    which = lax.broadcasted_iota(jnp.int32, (experts, tokens), 0)
    first, second = which == ids[0:1], which == ids[1:2]
    named = jnp.where(first | second, 1.0, 0.0).astype(jnp.bfloat16)
    before = lax.broadcasted_iota(jnp.int32, (tokens, tokens), 0) < lax.broadcasted_iota(
        jnp.int32, (tokens, tokens), 1
    )
    earlier = matmul(named, jnp.where(before, 1.0, 0.0).astype(jnp.bfloat16), NN)
    return [
        jnp.sum(jnp.where(mine, earlier, 0.0), axis=0, keepdims=True).astype(jnp.int32)
        for mine in (first, second)
    ]


def pick_rows(ids, slot, rows, per_peer, rest):
    shift = rest.bit_length() - 1
    half = lax.axis_index("half")
    row = lax.broadcasted_iota(jnp.int32, (rows, ids.shape[1]), 0)
    hits = []
    for k in range(2):
        e = ids[k : k + 1]
        peer = ((e >> (shift + 1)) << shift) | (e & (rest - 1))
        mine = ((e >> shift) & 1) == half
        hits.append(row == jnp.where(mine, peer * per_peer + slot[k], -1))
    return jnp.where(hits[0] | hits[1], 1.0, 0.0).astype(jnp.bfloat16)


def route_body(experts, per_peer, rest, ids_ref, tok_ref, send_ref, target_ref, late_ref):
    ids = ids_ref[...]
    slot = slots(ids, experts)
    for k in range(2):
        target_ref[k : k + 1, :] = ids[k : k + 1] * per_peer + slot[k]
    late_ref[...] = tok_ref[tok_ref.shape[0] - late_ref.shape[0] :, :]
    near_pick = pick_rows(ids, slot, send_ref.shape[0], per_peer, rest)
    send_ref[...] = matmul(near_pick, tok_ref[...], NN).astype(jnp.bfloat16)


def route(ids, tokens, early, experts, per_peer, rest):
    rows, width = experts // 2 * per_peer, tokens.shape[1]
    return pl.pallas_call(
        functools.partial(route_body, experts, per_peer, rest),
        out_shape=(
            jax.ShapeDtypeStruct((rows, width), jnp.bfloat16),
            jax.ShapeDtypeStruct(ids.shape, jnp.int32),
            jax.ShapeDtypeStruct((tokens.shape[0] - early, width), jnp.bfloat16),
        ),
        cost_estimate=pl.CostEstimate(
            flops=2 * rows * tokens.shape[0] * width,
            bytes_accessed=2 * (rows + tokens.shape[0]) * width,
            transcendentals=0,
        ),
        compiler_params=pltpu.CompilerParams(vmem_limit_bytes=60 << 20),
        name="route",
    )(ids, tokens)


def gather_first_body(experts, per_peer, rest, ids_ref, tok_ref, part_ref, pick_ref):
    ids = ids_ref[...]
    pick = pick_rows(ids, slots(ids, experts), part_ref.shape[0], per_peer, rest)
    count = tok_ref.shape[0]
    part_ref[...] = matmul(pick[:, :count], tok_ref[...], NN).astype(jnp.bfloat16)
    pick_ref[...] = pick[:, count:]


def gather_first(ids, tokens, experts, per_peer, rest):
    rows, width = experts // 2 * per_peer, tokens.shape[1]
    return pl.pallas_call(
        functools.partial(gather_first_body, experts, per_peer, rest),
        out_shape=(
            jax.ShapeDtypeStruct((rows, width), jnp.bfloat16),
            jax.ShapeDtypeStruct((rows, ids.shape[1] - tokens.shape[0]), jnp.bfloat16),
        ),
        compiler_params=pltpu.CompilerParams(vmem_limit_bytes=SMALL),
        cost_estimate=pl.CostEstimate(flops=40 * 10**9, bytes_accessed=0, transcendentals=0),
        name="gather_first",
    )(ids, tokens)


def gather_last_body(pick_ref, tok_ref, part_ref, send_ref):
    rows = matmul(pick_ref[...], tok_ref[...], NN) + part_ref[...].astype(jnp.float32)
    send_ref[...] = rows.astype(jnp.bfloat16)


def gather_last(pick, tokens, part):
    rows, count = pick.shape
    return pl.pallas_call(
        gather_last_body,
        out_shape=jax.ShapeDtypeStruct(part.shape, jnp.bfloat16),
        compiler_params=pltpu.CompilerParams(vmem_limit_bytes=SMALL),
        cost_estimate=pl.CostEstimate(
            flops=2 * rows * count * part.shape[1], bytes_accessed=0, transcendentals=0
        ),
        name="gather_last",
    )(pick, tokens, part)


def expert_body(blocks, packed, far, *refs):
    x_hbm, p_hbm, wo_hbm, wi_hbm = refs[:4]
    near_hbm = refs[4] if far else None
    o_ref, x, p, wo, wi, acc, gsum, sem = refs[4 + far :]
    rows, width = x.shape
    size = wo.shape[1]
    own = lax.axis_index("half")
    half = 1 - own if far else own

    def up(j):
        return pltpu.make_async_copy(wo_hbm.at[pl.ds(j * size, size), :], wo.at[j], sem.at[0, j])

    def pre(j):
        return pltpu.make_async_copy(
            p_hbm.at[:, half, :, pl.ds(j * size, size)], p.at[j], sem.at[1, j]
        )

    def down(j):
        return pltpu.make_async_copy(wi_hbm.at[:, pl.ds(j * size, size)], wi.at[j], sem.at[2, j])

    rows_in = pltpu.make_async_copy(x_hbm, x, sem.at[3, 0])
    rows_in.start()
    for j in range(blocks):
        up(j).start()
        pre(j).start()
        down(j).start()
    if far:
        near = pltpu.make_async_copy(near_hbm, o_ref.at[:, own], sem.at[3, 1])
        near.start()
    rows_in.wait()
    up(0).wait()
    upstream = matmul(x[...], wo[0], NT)
    for j in range(blocks):
        pre(j).wait()
        down(j).wait()
        following = None
        if j + 1 < blocks:
            up(j + 1).wait()
            following = matmul(x[...], wo[j + 1], NT)
        act = p[j].astype(jnp.float32).reshape(rows, size)
        prod = jnp.maximum(act, 0.0) * upstream
        part = prod[:, :LANES]
        for q in range(1, size // LANES):
            part = part + prod[:, q * LANES : (q + 1) * LANES]
        hidden = jnp.where(act > 0, upstream, 0.0).astype(jnp.bfloat16)
        back = matmul(hidden, wi[j], NT)
        if j == 0:
            acc[...] = back
            gsum[...] = part
        else:
            acc[...] += back
            gsum[...] += part
        upstream = following
    dots = jnp.sum(gsum[...], axis=1, keepdims=True)
    high = dots.astype(jnp.bfloat16).astype(jnp.float32)
    low = dots - high
    out = acc[...].astype(jnp.bfloat16)
    if far:
        near.wait()
    dst = o_ref.at[:, half] if far else o_ref
    if not packed:
        lane = lax.broadcasted_iota(jnp.int32, (rows, LANES), 1)
        tail = jnp.where(lane == 0, high, jnp.where(lane == 1, low, 0.0)).astype(jnp.bfloat16)
        dst[:, :, :width] = out.reshape(*dst.shape[:2], width)
        dst[:, :, width:] = tail.reshape(*dst.shape[:2], LANES)
        return
    outer, rest = dst.shape[:2]
    peers = outer * rest
    groups, cols = rows // peers // SUBLANES, width // LANES
    lane = lax.broadcasted_iota(jnp.int32, (peers, SUBLANES, LANES), 2)
    out = out.reshape(peers, groups, SUBLANES, width)
    high = high.reshape(peers, groups, SUBLANES, 1)
    low = low.reshape(peers, groups, SUBLANES, 1)
    tail = jnp.zeros((peers, SUBLANES, LANES), jnp.float32)
    for r in range(groups):
        tail = jnp.where(lane == 2 * r, high[:, r], tail)
        tail = jnp.where(lane == 2 * r + 1, low[:, r], tail)
        for c in range(cols):
            at = (r * cols + c) * SUBLANES
            dst[:, :, at : at + SUBLANES, :] = out[:, r, :, c * LANES : (c + 1) * LANES].reshape(
                outer, rest, SUBLANES, LANES
            )
    dst[:, :, groups * cols * SUBLANES :, :] = tail.astype(jnp.bfloat16).reshape(
        outer, rest, SUBLANES, LANES
    )


def expert(x, p, wo, wi, rest, blocks, near=None):
    rows, width = x.shape
    outer, _, group, hidden = p.shape
    size = hidden // blocks
    per_peer = group // rest
    far = near is not None
    packed = per_peer % SUBLANES == 0
    both = (2,) if far else ()
    shape = (
        (outer, *both, rest, per_peer * (width // LANES) + SUBLANES, LANES)
        if packed
        else (outer, *both, group, width + LANES)
    )
    operands = (x, p, wo, wi) + ((near,) if far else ())
    return pl.pallas_call(
        functools.partial(expert_body, blocks, packed, int(far)),
        out_shape=jax.ShapeDtypeStruct(shape, jnp.bfloat16),
        in_specs=[
            pl.BlockSpec(memory_space=pltpu.HBM if 1 <= i <= 3 else pl.ANY)
            for i in range(len(operands))
        ],
        out_specs=pl.BlockSpec(memory_space=pltpu.VMEM),
        scratch_shapes=[
            pltpu.VMEM((rows, width), jnp.bfloat16),
            pltpu.VMEM((blocks, outer, group, size), jnp.bfloat16),
            pltpu.VMEM((blocks, size, width), jnp.bfloat16),
            pltpu.VMEM((blocks, width, size), jnp.bfloat16),
            pltpu.VMEM((rows, width), jnp.float32),
            pltpu.VMEM((rows, LANES), jnp.float32),
            pltpu.SemaphoreType.DMA((4, blocks)),
        ],
        compiler_params=pltpu.CompilerParams(vmem_limit_bytes=50 << 20),
        cost_estimate=pl.CostEstimate(
            flops=4 * rows * width * hidden,
            bytes_accessed=2 * (rows * hidden + 2 * width * hidden + 2 * rows * width),
            transcendentals=0,
        ),
        name="expert_far" if far else "expert_near",
    )(*operands)


def combine_body(packed, target_ref, gate_ref, back_ref, grad_ref, dots_ref):
    tokens, width = grad_ref.shape
    if packed:
        peers = back_ref.shape[0]
        cols = width // LANES
        groups = back_ref.shape[1] // SUBLANES // cols
        rows = peers * groups * SUBLANES
    else:
        rows = back_ref.shape[0]
    row = lax.broadcasted_iota(jnp.int32, (rows, tokens), 0)
    hit = [row == target_ref[k : k + 1, :] for k in range(2)]
    weight = jnp.where(
        hit[0], gate_ref[0:1, :], jnp.where(hit[1], gate_ref[1:2, :], 0.0)
    )
    high = weight.astype(jnp.bfloat16)
    low = (weight - high.astype(jnp.float32)).astype(jnp.bfloat16)
    if packed:

        def column(c):
            return jnp.stack(
                [
                    back_ref[:, (r * cols + c) * SUBLANES : (r * cols + c + 1) * SUBLANES, :]
                    for r in range(groups)
                ],
                axis=1,
            ).reshape(rows, LANES)

        tail = back_ref[:, groups * cols * SUBLANES :, :].astype(jnp.float32)
        lane = lax.broadcasted_iota(jnp.int32, tail.shape, 2)
        sums = (
            jnp.stack([jnp.where(lane // 2 == r, tail, 0.0) for r in range(groups)], axis=1)
            .reshape(rows, LANES)
            .astype(jnp.bfloat16)
        )
        for c in range(0, cols, 2):
            part = jnp.concatenate([column(c), column(c + 1)], axis=1)
            grad_ref[:, c * LANES : (c + 2) * LANES] = (
                matmul(high, part, TN) + matmul(low, part, TN)
            ).astype(jnp.bfloat16)
    else:
        part = back_ref[:, :width]
        grad_ref[...] = (matmul(high, part, TN) + matmul(low, part, TN)).astype(jnp.bfloat16)
        sums = back_ref[:, width:]
    for k in range(2):
        pick = jnp.where(hit[k], 1.0, 0.0).astype(jnp.bfloat16)
        dots_ref[k : k + 1, :] = jnp.sum(matmul(sums, pick, TN), axis=0, keepdims=True)


def combine(target, gates, back, width):
    tokens = gates.shape[1]
    packed = back.ndim == 3
    return pl.pallas_call(
        functools.partial(combine_body, packed),
        out_shape=(
            jax.ShapeDtypeStruct((tokens, width), jnp.bfloat16),
            jax.ShapeDtypeStruct(gates.shape, jnp.float32),
        ),
        compiler_params=pltpu.CompilerParams(vmem_limit_bytes=16 << 20),
        name="combine",
    )(target, gates, back)


def per_device(output_grad, expert_ids, gate_weights, pre_act, w_in, w_out):
    outer, rest = lax.axis_size("outer"), lax.axis_size("rest")
    devices = 2 * outer * rest
    width = output_grad.shape[1]
    cap_rows, hidden = pre_act.shape[1:]
    per_peer = cap_rows // devices
    group = rest * per_peer
    swap = [(0, 1), (1, 0)]

    def exchange(x, axes):
        return lax.all_to_all(x, axes, split_axis=0, concat_axis=0, tiled=True)

    def to_half(rows):
        peers = rows.reshape(outer * rest, per_peer, width)
        return exchange(peers, ("outer", "rest")).reshape(outer * group, width)

    ids = expert_ids.T
    far_ids = lax.ppermute(ids, "half", swap)
    early = output_grad.shape[0] // 2
    first = lax.ppermute(output_grad[:early], "half", swap)
    send, target, late = route(ids, output_grad, early, devices, per_peer, rest)
    second = lax.ppermute(late, "half", swap)
    near_rows = to_half(send)
    part, pick = gather_first(far_ids, first, devices, per_peer, rest)
    far_rows = to_half(gather_last(pick, second, part))
    act = pre_act.reshape(outer, 2, group, hidden)
    near = expert(near_rows, act, w_out[0], w_in[0], rest, 4)
    result = expert(far_rows, act, w_out[0], w_in[0], rest, 4, near)
    if result.ndim == 5:
        result = result.reshape(devices, *result.shape[3:])
    else:
        result = result.reshape(devices, per_peer, -1)
    back = exchange(result, ("outer", "half", "rest"))
    if per_peer % SUBLANES:
        back = back.reshape(cap_rows, -1)
    input_grad, gate_grad = combine(target, gate_weights.T, back, width)
    return input_grad, gate_grad.T


def solution(mesh):
    outer, inner = mesh.shape["outer"], mesh.shape["inner"]
    split = jax.sharding.Mesh(
        mesh.devices.reshape(outer, 2, inner // 2), ("outer", "half", "rest")
    )
    axes = ("outer", "half", "rest")
    rows, blocks = P(axes, None), P(axes, None, None)
    return jax.shard_map(
        per_device,
        mesh=split,
        in_specs=(rows, rows, rows, blocks, blocks, blocks),
        out_specs=(rows, rows),
        check_vma=False,
    )
```

```python
import functools

import jax
import jax.numpy as jnp
from jax import lax
from jax.experimental import pallas as pl
from jax.experimental.pallas import tpu as pltpu
from jax.sharding import PartitionSpec as P

LANES = 128
SUBLANES = 8
SMALL = 8 << 20
PARTS = (2, 2, 4, 4, 4)
NN = (((1,), (0,)), ((), ()))
NT = (((1,), (1,)), ((), ()))
TN = (((0,), (0,)), ((), ()))


def matmul(a, b, dims):
    return lax.dot_general(a, b, dims, preferred_element_type=jnp.float32)


def slots(ids, experts):
    tokens = ids.shape[1]
    which = lax.broadcasted_iota(jnp.int32, (experts, tokens), 0)
    first, second = which == ids[0:1], which == ids[1:2]
    named = jnp.where(first | second, 1.0, 0.0).astype(jnp.bfloat16)
    before = lax.broadcasted_iota(jnp.int32, (tokens, tokens), 0) < lax.broadcasted_iota(
        jnp.int32, (tokens, tokens), 1
    )
    earlier = matmul(named, jnp.where(before, 1.0, 0.0).astype(jnp.bfloat16), NN)
    return [
        jnp.sum(jnp.where(mine, earlier, 0.0), axis=0, keepdims=True).astype(jnp.int32)
        for mine in (first, second)
    ]


def pick_rows(ids, slot, rows, per_peer, rest):
    shift = rest.bit_length() - 1
    half = lax.axis_index("half")
    row = lax.broadcasted_iota(jnp.int32, (rows, ids.shape[1]), 0)
    hits = []
    for k in range(2):
        e = ids[k : k + 1]
        peer = ((e >> (shift + 1)) << shift) | (e & (rest - 1))
        mine = ((e >> shift) & 1) == half
        hits.append(row == jnp.where(mine, peer * per_peer + slot[k], -1))
    return jnp.where(hits[0] | hits[1], 1.0, 0.0).astype(jnp.bfloat16)


def route_body(experts, per_peer, rest, ids_ref, tok_ref, send_ref, target_ref, late_ref):
    ids = ids_ref[...]
    slot = slots(ids, experts)
    for k in range(2):
        target_ref[k : k + 1, :] = ids[k : k + 1] * per_peer + slot[k]
    late_ref[...] = tok_ref[tok_ref.shape[0] - late_ref.shape[0] :, :]
    near_pick = pick_rows(ids, slot, send_ref.shape[0], per_peer, rest)
    send_ref[...] = matmul(near_pick, tok_ref[...], NN).astype(jnp.bfloat16)


def route(ids, tokens, early, experts, per_peer, rest):
    rows, width = experts // 2 * per_peer, tokens.shape[1]
    return pl.pallas_call(
        functools.partial(route_body, experts, per_peer, rest),
        out_shape=(
            jax.ShapeDtypeStruct((rows, width), jnp.bfloat16),
            jax.ShapeDtypeStruct(ids.shape, jnp.int32),
            jax.ShapeDtypeStruct((tokens.shape[0] - early, width), jnp.bfloat16),
        ),
        cost_estimate=pl.CostEstimate(
            flops=2 * rows * tokens.shape[0] * width,
            bytes_accessed=2 * (rows + tokens.shape[0]) * width,
            transcendentals=0,
        ),
        compiler_params=pltpu.CompilerParams(vmem_limit_bytes=60 << 20),
        name="route",
    )(ids, tokens)


def gather_first_body(experts, per_peer, rest, ids_ref, tok_ref, part_ref, pick_ref):
    ids = ids_ref[...]
    pick = pick_rows(ids, slots(ids, experts), part_ref.shape[0], per_peer, rest)
    count = tok_ref.shape[0]
    part_ref[...] = matmul(pick[:, :count], tok_ref[...], NN).astype(jnp.bfloat16)
    pick_ref[...] = pick[:, count:]


def gather_first(ids, tokens, experts, per_peer, rest):
    rows, width = experts // 2 * per_peer, tokens.shape[1]
    return pl.pallas_call(
        functools.partial(gather_first_body, experts, per_peer, rest),
        out_shape=(
            jax.ShapeDtypeStruct((rows, width), jnp.bfloat16),
            jax.ShapeDtypeStruct((rows, ids.shape[1] - tokens.shape[0]), jnp.bfloat16),
        ),
        compiler_params=pltpu.CompilerParams(vmem_limit_bytes=SMALL),
        cost_estimate=pl.CostEstimate(flops=40 * 10**9, bytes_accessed=0, transcendentals=0),
        name="gather_first",
    )(ids, tokens)


def gather_last_body(pick_ref, tok_ref, part_ref, send_ref):
    rows = matmul(pick_ref[...], tok_ref[...], NN) + part_ref[...].astype(jnp.float32)
    send_ref[...] = rows.astype(jnp.bfloat16)


def gather_last(pick, tokens, part):
    rows, count = pick.shape
    return pl.pallas_call(
        gather_last_body,
        out_shape=jax.ShapeDtypeStruct(part.shape, jnp.bfloat16),
        compiler_params=pltpu.CompilerParams(vmem_limit_bytes=SMALL),
        cost_estimate=pl.CostEstimate(
            flops=2 * rows * count * part.shape[1], bytes_accessed=0, transcendentals=0
        ),
        name="gather_last",
    )(pick, tokens, part)


def expert_body(sizes, packed, far, *refs):
    x_hbm, p_hbm, wo_hbm, wi_hbm = refs[:4]
    near_hbm = refs[4] if far else None
    o_ref, x, acc, gsum, sem, *bufs = refs[4 + far :]
    rows, width = x.shape
    blocks = len(sizes)
    p, wo, wi = bufs[:blocks], bufs[blocks : 2 * blocks], bufs[2 * blocks :]
    own = lax.axis_index("half")
    half = 1 - own if far else own

    def block(j):
        return pl.ds(sum(sizes[:j]), sizes[j])

    def up(j):
        return pltpu.make_async_copy(wo_hbm.at[block(j), :], wo[j], sem.at[0, j])

    def pre(j):
        return pltpu.make_async_copy(p_hbm.at[:, half, :, block(j)], p[j], sem.at[1, j])

    def down(j):
        return pltpu.make_async_copy(wi_hbm.at[:, block(j)], wi[j], sem.at[2, j])

    rows_in = pltpu.make_async_copy(x_hbm, x, sem.at[3, 0])
    rows_in.start()
    for j in range(blocks):
        up(j).start()
        pre(j).start()
        down(j).start()
    if far:
        near = pltpu.make_async_copy(near_hbm, o_ref.at[:, own], sem.at[3, 1])
        near.start()
    rows_in.wait()
    up(0).wait()
    upstream = matmul(x[...], wo[0][...], NT)
    for j in range(blocks):
        pre(j).wait()
        down(j).wait()
        following = None
        if j + 1 < blocks:
            up(j + 1).wait()
            following = matmul(x[...], wo[j + 1][...], NT)
        act = p[j][...].astype(jnp.float32).reshape(rows, sizes[j])
        prod = jnp.maximum(act, 0.0) * upstream
        part = prod[:, :LANES]
        for q in range(1, sizes[j] // LANES):
            part = part + prod[:, q * LANES : (q + 1) * LANES]
        hidden = jnp.where(act > 0, upstream, 0.0).astype(jnp.bfloat16)
        back = matmul(hidden, wi[j][...], NT)
        if j == 0:
            acc[...] = back
            gsum[...] = part
        else:
            acc[...] += back
            gsum[...] += part
        upstream = following
    dots = jnp.sum(gsum[...], axis=1, keepdims=True)
    high = dots.astype(jnp.bfloat16).astype(jnp.float32)
    low = dots - high
    out = acc[...].astype(jnp.bfloat16)
    if far:
        near.wait()
    dst = o_ref.at[:, half] if far else o_ref
    if not packed:
        lane = lax.broadcasted_iota(jnp.int32, (rows, LANES), 1)
        tail = jnp.where(lane == 0, high, jnp.where(lane == 1, low, 0.0)).astype(jnp.bfloat16)
        dst[:, :, :width] = out.reshape(*dst.shape[:2], width)
        dst[:, :, width:] = tail.reshape(*dst.shape[:2], LANES)
        return
    outer, rest = dst.shape[:2]
    peers = outer * rest
    groups, cols = rows // peers // SUBLANES, width // LANES
    lane = lax.broadcasted_iota(jnp.int32, (peers, SUBLANES, LANES), 2)
    out = out.reshape(peers, groups, SUBLANES, width)
    high = high.reshape(peers, groups, SUBLANES, 1)
    low = low.reshape(peers, groups, SUBLANES, 1)
    tail = jnp.zeros((peers, SUBLANES, LANES), jnp.float32)
    for r in range(groups):
        tail = jnp.where(lane == 2 * r, high[:, r], tail)
        tail = jnp.where(lane == 2 * r + 1, low[:, r], tail)
        for c in range(cols):
            at = (r * cols + c) * SUBLANES
            dst[:, :, at : at + SUBLANES, :] = out[:, r, :, c * LANES : (c + 1) * LANES].reshape(
                outer, rest, SUBLANES, LANES
            )
    dst[:, :, groups * cols * SUBLANES :, :] = tail.astype(jnp.bfloat16).reshape(
        outer, rest, SUBLANES, LANES
    )


def expert(x, p, wo, wi, rest, near=None):
    rows, width = x.shape
    outer, _, group, hidden = p.shape
    sizes = [part * hidden // sum(PARTS) for part in PARTS]
    per_peer = group // rest
    far = near is not None
    packed = per_peer % SUBLANES == 0
    both = (2,) if far else ()
    shape = (
        (outer, *both, rest, per_peer * (width // LANES) + SUBLANES, LANES)
        if packed
        else (outer, *both, group, width + LANES)
    )
    operands = (x, p, wo, wi) + ((near,) if far else ())
    return pl.pallas_call(
        functools.partial(expert_body, sizes, packed, int(far)),
        out_shape=jax.ShapeDtypeStruct(shape, jnp.bfloat16),
        in_specs=[pl.BlockSpec(memory_space=pl.ANY)] * len(operands),
        out_specs=pl.BlockSpec(memory_space=pltpu.VMEM),
        scratch_shapes=[
            pltpu.VMEM((rows, width), jnp.bfloat16),
            pltpu.VMEM((rows, width), jnp.float32),
            pltpu.VMEM((rows, LANES), jnp.float32),
            pltpu.SemaphoreType.DMA((4, len(sizes))),
        ]
        + [pltpu.VMEM((outer, group, size), jnp.bfloat16) for size in sizes]
        + [pltpu.VMEM((size, width), jnp.bfloat16) for size in sizes]
        + [pltpu.VMEM((width, size), jnp.bfloat16) for size in sizes],
        compiler_params=pltpu.CompilerParams(vmem_limit_bytes=50 << 20),
        cost_estimate=pl.CostEstimate(
            flops=4 * rows * width * hidden,
            bytes_accessed=2 * (rows * hidden + 2 * width * hidden + 2 * rows * width),
            transcendentals=0,
        ),
        name="expert_far" if far else "expert_near",
    )(*operands)


def combine_body(packed, target_ref, gate_ref, back_ref, grad_ref, dots_ref):
    tokens, width = grad_ref.shape
    if packed:
        peers = back_ref.shape[0]
        cols = width // LANES
        groups = back_ref.shape[1] // SUBLANES // cols
        rows = peers * groups * SUBLANES
    else:
        rows = back_ref.shape[0]
    row = lax.broadcasted_iota(jnp.int32, (rows, tokens), 0)
    hit = [row == target_ref[k : k + 1, :] for k in range(2)]
    weight = jnp.where(
        hit[0], gate_ref[0:1, :], jnp.where(hit[1], gate_ref[1:2, :], 0.0)
    )
    weight = weight.astype(jnp.bfloat16)
    if packed:

        def column(c):
            return jnp.stack(
                [
                    back_ref[:, (r * cols + c) * SUBLANES : (r * cols + c + 1) * SUBLANES, :]
                    for r in range(groups)
                ],
                axis=1,
            ).reshape(rows, LANES)

        tail = back_ref[:, groups * cols * SUBLANES :, :].astype(jnp.float32)
        lane = lax.broadcasted_iota(jnp.int32, tail.shape, 2)
        sums = (
            jnp.stack([jnp.where(lane // 2 == r, tail, 0.0) for r in range(groups)], axis=1)
            .reshape(rows, LANES)
            .astype(jnp.bfloat16)
        )
        for c in range(0, cols, 2):
            part = jnp.concatenate([column(c), column(c + 1)], axis=1)
            grad_ref[:, c * LANES : (c + 2) * LANES] = matmul(weight, part, TN).astype(
                jnp.bfloat16
            )
    else:
        part = back_ref[:, :width]
        grad_ref[...] = matmul(weight, part, TN).astype(jnp.bfloat16)
        sums = back_ref[:, width:]
    for k in range(2):
        pick = jnp.where(hit[k], 1.0, 0.0).astype(jnp.bfloat16)
        dots_ref[k : k + 1, :] = jnp.sum(matmul(sums, pick, TN), axis=0, keepdims=True)


def combine(target, gates, back, width):
    tokens = gates.shape[1]
    packed = back.ndim == 3
    return pl.pallas_call(
        functools.partial(combine_body, packed),
        out_shape=(
            jax.ShapeDtypeStruct((tokens, width), jnp.bfloat16),
            jax.ShapeDtypeStruct(gates.shape, jnp.float32),
        ),
        compiler_params=pltpu.CompilerParams(vmem_limit_bytes=16 << 20),
        name="combine",
    )(target, gates, back)


def per_device(output_grad, expert_ids, gate_weights, pre_act, w_in, w_out):
    outer, rest = lax.axis_size("outer"), lax.axis_size("rest")
    devices = 2 * outer * rest
    width = output_grad.shape[1]
    cap_rows, hidden = pre_act.shape[1:]
    per_peer = cap_rows // devices
    group = rest * per_peer
    swap = [(0, 1), (1, 0)]

    def exchange(x, axes):
        return lax.all_to_all(x, axes, split_axis=0, concat_axis=0, tiled=True)

    def to_half(rows):
        peers = rows.reshape(outer * rest, per_peer, width)
        return exchange(peers, ("outer", "rest")).reshape(outer * group, width)

    ids = expert_ids.T
    far_ids = lax.ppermute(ids, "half", swap)
    early = output_grad.shape[0] // 2
    first = lax.ppermute(output_grad[:early], "half", swap)
    send, target, late = route(ids, output_grad, early, devices, per_peer, rest)
    second = lax.ppermute(late, "half", swap)
    near_rows = to_half(send)
    part, pick = gather_first(far_ids, first, devices, per_peer, rest)
    far_rows = to_half(gather_last(pick, second, part))
    act = pre_act.reshape(outer, 2, group, hidden)
    near = expert(near_rows, act, w_out[0], w_in[0], rest)
    result = expert(far_rows, act, w_out[0], w_in[0], rest, near)
    if result.ndim == 5:
        result = result.reshape(devices, *result.shape[3:])
    else:
        result = result.reshape(devices, per_peer, -1)
    back = exchange(result, ("outer", "half", "rest"))
    if per_peer % SUBLANES:
        back = back.reshape(cap_rows, -1)
    input_grad, gate_grad = combine(target, gate_weights.T, back, width)
    return input_grad, gate_grad.T


def solution(mesh):
    outer, inner = mesh.shape["outer"], mesh.shape["inner"]
    split = jax.sharding.Mesh(
        mesh.devices.reshape(outer, 2, inner // 2), ("outer", "half", "rest")
    )
    axes = ("outer", "half", "rest")
    rows, blocks = P(axes, None), P(axes, None, None)
    return jax.shard_map(
        per_device,
        mesh=split,
        in_specs=(rows, rows, rows, blocks, blocks, blocks),
        out_specs=(rows, rows),
        check_vma=False,
    )
```

```python
import functools

import jax
import jax.numpy as jnp
from jax import lax
from jax.experimental import pallas as pl
from jax.experimental.pallas import tpu as pltpu
from jax.sharding import PartitionSpec as P

LANES = 128
SUBLANES = 8
SMALL = 8 << 20
PARTS = (2, 2, 4, 4, 4)
NN = (((1,), (0,)), ((), ()))
NT = (((1,), (1,)), ((), ()))
TN = (((0,), (0,)), ((), ()))


def matmul(a, b, dims):
    return lax.dot_general(a, b, dims, preferred_element_type=jnp.float32)


def slots(ids, experts):
    tokens = ids.shape[1]
    which = lax.broadcasted_iota(jnp.int32, (experts, tokens), 0)
    first, second = which == ids[0:1], which == ids[1:2]
    named = jnp.where(first | second, 1.0, 0.0).astype(jnp.bfloat16)
    before = lax.broadcasted_iota(jnp.int32, (tokens, tokens), 0) < lax.broadcasted_iota(
        jnp.int32, (tokens, tokens), 1
    )
    earlier = matmul(named, jnp.where(before, 1.0, 0.0).astype(jnp.bfloat16), NN)
    return [
        jnp.sum(jnp.where(mine, earlier, 0.0), axis=0, keepdims=True).astype(jnp.int32)
        for mine in (first, second)
    ]


def pick_rows(ids, slot, rows, per_peer, rest):
    shift = rest.bit_length() - 1
    half = lax.axis_index("half")
    row = lax.broadcasted_iota(jnp.int32, (rows, ids.shape[1]), 0)
    hits = []
    for k in range(2):
        e = ids[k : k + 1]
        peer = ((e >> (shift + 1)) << shift) | (e & (rest - 1))
        mine = ((e >> shift) & 1) == half
        hits.append(row == jnp.where(mine, peer * per_peer + slot[k], -1))
    return jnp.where(hits[0] | hits[1], 1.0, 0.0).astype(jnp.bfloat16)


def route_body(experts, per_peer, rest, ids_ref, tok_ref, send_ref, target_ref, late_ref):
    ids = ids_ref[...]
    slot = slots(ids, experts)
    for k in range(2):
        target_ref[k : k + 1, :] = ids[k : k + 1] * per_peer + slot[k]
    late_ref[...] = tok_ref[tok_ref.shape[0] - late_ref.shape[0] :, :]
    near_pick = pick_rows(ids, slot, send_ref.shape[0], per_peer, rest)
    send_ref[...] = matmul(near_pick, tok_ref[...], NN).astype(jnp.bfloat16)


def route(ids, tokens, early, experts, per_peer, rest):
    rows, width = experts // 2 * per_peer, tokens.shape[1]
    return pl.pallas_call(
        functools.partial(route_body, experts, per_peer, rest),
        out_shape=(
            jax.ShapeDtypeStruct((rows, width), jnp.bfloat16),
            jax.ShapeDtypeStruct(ids.shape, jnp.int32),
            jax.ShapeDtypeStruct((tokens.shape[0] - early, width), jnp.bfloat16),
        ),
        cost_estimate=pl.CostEstimate(
            flops=2 * rows * tokens.shape[0] * width,
            bytes_accessed=2 * (rows + tokens.shape[0]) * width,
            transcendentals=0,
        ),
        compiler_params=pltpu.CompilerParams(vmem_limit_bytes=60 << 20),
        name="route",
    )(ids, tokens)


def gather_first_body(experts, per_peer, rest, ids_ref, tok_ref, part_ref, pick_ref):
    ids = ids_ref[...]
    pick = pick_rows(ids, slots(ids, experts), part_ref.shape[0], per_peer, rest)
    count = tok_ref.shape[0]
    part_ref[...] = matmul(pick[:, :count], tok_ref[...], NN).astype(jnp.bfloat16)
    pick_ref[...] = pick[:, count:]


def gather_first(ids, tokens, experts, per_peer, rest):
    rows, width = experts // 2 * per_peer, tokens.shape[1]
    return pl.pallas_call(
        functools.partial(gather_first_body, experts, per_peer, rest),
        out_shape=(
            jax.ShapeDtypeStruct((rows, width), jnp.bfloat16),
            jax.ShapeDtypeStruct((rows, ids.shape[1] - tokens.shape[0]), jnp.bfloat16),
        ),
        compiler_params=pltpu.CompilerParams(vmem_limit_bytes=SMALL),
        cost_estimate=pl.CostEstimate(flops=40 * 10**9, bytes_accessed=0, transcendentals=0),
        name="gather_first",
    )(ids, tokens)


def gather_last_body(pick_ref, tok_ref, part_ref, send_ref):
    rows = matmul(pick_ref[...], tok_ref[...], NN) + part_ref[...].astype(jnp.float32)
    send_ref[...] = rows.astype(jnp.bfloat16)


def gather_last(pick, tokens, part):
    rows, count = pick.shape
    return pl.pallas_call(
        gather_last_body,
        out_shape=jax.ShapeDtypeStruct(part.shape, jnp.bfloat16),
        compiler_params=pltpu.CompilerParams(vmem_limit_bytes=SMALL),
        cost_estimate=pl.CostEstimate(
            flops=2 * rows * count * part.shape[1], bytes_accessed=0, transcendentals=0
        ),
        name="gather_last",
    )(pick, tokens, part)


def expert_body(sizes, packed, far, *refs):
    x_hbm, p_hbm, wo_hbm, wi_hbm = refs[:4]
    near_hbm = refs[4] if far else None
    o_ref, x, acc, gsum, sem, *bufs = refs[4 + far :]
    rows, width = x.shape
    blocks = len(sizes)
    p, wo, wi = bufs[:blocks], bufs[blocks : 2 * blocks], bufs[2 * blocks :]
    own = lax.axis_index("half")
    half = 1 - own if far else own

    def block(j):
        return pl.ds(sum(sizes[:j]), sizes[j])

    def up(j):
        return pltpu.make_async_copy(wo_hbm.at[block(j), :], wo[j], sem.at[0, j])

    def pre(j):
        return pltpu.make_async_copy(p_hbm.at[:, half, :, block(j)], p[j], sem.at[1, j])

    def down(j):
        return pltpu.make_async_copy(wi_hbm.at[:, block(j)], wi[j], sem.at[2, j])

    rows_in = pltpu.make_async_copy(x_hbm, x, sem.at[3, 0])
    rows_in.start()
    for j in range(blocks):
        up(j).start()
        pre(j).start()
        down(j).start()
    if far:
        near = pltpu.make_async_copy(near_hbm, o_ref.at[:, own], sem.at[3, 1])
        near.start()
    rows_in.wait()
    up(0).wait()
    upstream = matmul(x[...], wo[0][...], NT)
    for j in range(blocks):
        pre(j).wait()
        down(j).wait()
        following = None
        if j + 1 < blocks:
            up(j + 1).wait()
            following = matmul(x[...], wo[j + 1][...], NT)
        act = p[j][...].astype(jnp.float32).reshape(rows, sizes[j])
        prod = jnp.maximum(act, 0.0) * upstream
        part = prod[:, :LANES]
        for q in range(1, sizes[j] // LANES):
            part = part + prod[:, q * LANES : (q + 1) * LANES]
        hidden = jnp.where(act > 0, upstream, 0.0).astype(jnp.bfloat16)
        back = matmul(hidden, wi[j][...], NT)
        if j == 0:
            acc[...] = back
            gsum[...] = part
        else:
            acc[...] += back
            gsum[...] += part
        upstream = following
    dots = jnp.sum(gsum[...], axis=1, keepdims=True)
    high = dots.astype(jnp.bfloat16).astype(jnp.float32)
    low = dots - high
    out = acc[...].astype(jnp.bfloat16)
    if far:
        near.wait()
    dst = o_ref.at[:, half] if far else o_ref
    if not packed:
        lane = lax.broadcasted_iota(jnp.int32, (rows, LANES), 1)
        tail = jnp.where(lane == 0, high, jnp.where(lane == 1, low, 0.0)).astype(jnp.bfloat16)
        dst[:, :, :width] = out.reshape(*dst.shape[:2], width)
        dst[:, :, width:] = tail.reshape(*dst.shape[:2], LANES)
        return
    outer, rest = dst.shape[:2]
    peers = outer * rest
    groups, cols = rows // peers // SUBLANES, width // LANES
    lane = lax.broadcasted_iota(jnp.int32, (peers, SUBLANES, LANES), 2)
    out = out.reshape(peers, groups, SUBLANES, width)
    high = high.reshape(peers, groups, SUBLANES, 1)
    low = low.reshape(peers, groups, SUBLANES, 1)
    tail = jnp.zeros((peers, SUBLANES, LANES), jnp.float32)
    for r in range(groups):
        tail = jnp.where(lane == 2 * r, high[:, r], tail)
        tail = jnp.where(lane == 2 * r + 1, low[:, r], tail)
        for c in range(cols):
            at = (r * cols + c) * SUBLANES
            dst[:, :, at : at + SUBLANES, :] = out[:, r, :, c * LANES : (c + 1) * LANES].reshape(
                outer, rest, SUBLANES, LANES
            )
    dst[:, :, groups * cols * SUBLANES :, :] = tail.astype(jnp.bfloat16).reshape(
        outer, rest, SUBLANES, LANES
    )


def expert(x, p, wo, wi, rest, near=None):
    rows, width = x.shape
    outer, _, group, hidden = p.shape
    sizes = [part * hidden // sum(PARTS) for part in PARTS]
    per_peer = group // rest
    far = near is not None
    packed = per_peer % SUBLANES == 0
    both = (2,) if far else ()
    shape = (
        (outer, *both, rest, per_peer * (width // LANES) + SUBLANES, LANES)
        if packed
        else (outer, *both, group, width + LANES)
    )
    operands = (x, p, wo, wi) + ((near,) if far else ())
    return pl.pallas_call(
        functools.partial(expert_body, sizes, packed, int(far)),
        out_shape=jax.ShapeDtypeStruct(shape, jnp.bfloat16),
        in_specs=[pl.BlockSpec(memory_space=pl.ANY)] * len(operands),
        out_specs=pl.BlockSpec(memory_space=pltpu.VMEM),
        scratch_shapes=[
            pltpu.VMEM((rows, width), jnp.bfloat16),
            pltpu.VMEM((rows, width), jnp.float32),
            pltpu.VMEM((rows, LANES), jnp.float32),
            pltpu.SemaphoreType.DMA((4, len(sizes))),
        ]
        + [pltpu.VMEM((outer, group, size), jnp.bfloat16) for size in sizes]
        + [pltpu.VMEM((size, width), jnp.bfloat16) for size in sizes]
        + [pltpu.VMEM((width, size), jnp.bfloat16) for size in sizes],
        compiler_params=pltpu.CompilerParams(vmem_limit_bytes=50 << 20),
        cost_estimate=pl.CostEstimate(
            flops=4 * rows * width * hidden,
            bytes_accessed=2 * (rows * hidden + 2 * width * hidden + 2 * rows * width),
            transcendentals=0,
        ),
        name="expert_far" if far else "expert_near",
    )(*operands)


def combine_body(packed, target_ref, gate_ref, back_ref, grad_ref, dots_ref):
    tokens, width = grad_ref.shape
    if packed:
        peers = back_ref.shape[0]
        cols = width // LANES
        groups = back_ref.shape[1] // SUBLANES // cols
        rows = peers * groups * SUBLANES
    else:
        rows = back_ref.shape[0]
    row = lax.broadcasted_iota(jnp.int32, (rows, tokens), 0)
    hit = [row == target_ref[k : k + 1, :] for k in range(2)]
    weight = jnp.where(
        hit[0], gate_ref[0:1, :], jnp.where(hit[1], gate_ref[1:2, :], 0.0)
    )
    weight = weight.astype(jnp.bfloat16)
    if packed:

        def column(c):
            return jnp.stack(
                [
                    back_ref[:, (r * cols + c) * SUBLANES : (r * cols + c + 1) * SUBLANES, :]
                    for r in range(groups)
                ],
                axis=1,
            ).reshape(rows, LANES)

        tail = back_ref[:, groups * cols * SUBLANES :, :].astype(jnp.float32)
        lane = lax.broadcasted_iota(jnp.int32, tail.shape, 2)
        sums = (
            jnp.stack([jnp.where(lane // 2 == r, tail, 0.0) for r in range(groups)], axis=1)
            .reshape(rows, LANES)
            .astype(jnp.bfloat16)
        )
        for c in range(0, cols, 2):
            part = jnp.concatenate([column(c), column(c + 1)], axis=1)
            grad_ref[:, c * LANES : (c + 2) * LANES] = matmul(weight, part, TN).astype(
                jnp.bfloat16
            )
    else:
        part = back_ref[:, :width]
        grad_ref[...] = matmul(weight, part, TN).astype(jnp.bfloat16)
        sums = back_ref[:, width:]
    for k in range(2):
        pick = jnp.where(hit[k], 1.0, 0.0).astype(jnp.bfloat16)
        dots_ref[k : k + 1, :] = jnp.sum(matmul(sums, pick, TN), axis=0, keepdims=True)


def combine(target, gates, back, width):
    tokens = gates.shape[1]
    packed = back.ndim == 3
    return pl.pallas_call(
        functools.partial(combine_body, packed),
        out_shape=(
            jax.ShapeDtypeStruct((tokens, width), jnp.bfloat16),
            jax.ShapeDtypeStruct(gates.shape, jnp.float32),
        ),
        compiler_params=pltpu.CompilerParams(vmem_limit_bytes=16 << 20),
        name="combine",
    )(target, gates, back)


def per_device(output_grad, expert_ids, gate_weights, pre_act, w_in, w_out):
    outer, rest = lax.axis_size("outer"), lax.axis_size("rest")
    devices = 2 * outer * rest
    width = output_grad.shape[1]
    cap_rows, hidden = pre_act.shape[1:]
    per_peer = cap_rows // devices
    group = rest * per_peer
    swap = [(0, 1), (1, 0)]

    def exchange(x, axes):
        return lax.all_to_all(x, axes, split_axis=0, concat_axis=0, tiled=True)

    def to_half(rows):
        peers = rows.reshape(outer * rest, per_peer, width)
        return exchange(peers, ("outer", "rest")).reshape(outer * group, width)

    ids = expert_ids.T
    far_ids = lax.ppermute(ids, "half", swap)
    early = output_grad.shape[0] * 15 // 32
    first = lax.ppermute(output_grad[:early], "half", swap)
    send, target, late = route(ids, output_grad, early, devices, per_peer, rest)
    second = lax.ppermute(late, "half", swap)
    near_rows = to_half(send)
    part, pick = gather_first(far_ids, first, devices, per_peer, rest)
    far_rows = to_half(gather_last(pick, second, part))
    act = pre_act.reshape(outer, 2, group, hidden)
    near = expert(near_rows, act, w_out[0], w_in[0], rest)
    result = expert(far_rows, act, w_out[0], w_in[0], rest, near)
    if result.ndim == 5:
        result = result.reshape(devices, *result.shape[3:])
    else:
        result = result.reshape(devices, per_peer, -1)
    back = exchange(result, ("outer", "half", "rest"))
    if per_peer % SUBLANES:
        back = back.reshape(cap_rows, -1)
    input_grad, gate_grad = combine(target, gate_weights.T, back, width)
    return input_grad, gate_grad.T


def solution(mesh):
    outer, inner = mesh.shape["outer"], mesh.shape["inner"]
    split = jax.sharding.Mesh(
        mesh.devices.reshape(outer, 2, inner // 2), ("outer", "half", "rest")
    )
    axes = ("outer", "half", "rest")
    rows, blocks = P(axes, None), P(axes, None, None)
    return jax.shard_map(
        per_device,
        mesh=split,
        in_specs=(rows, rows, rows, blocks, blocks, blocks),
        out_specs=(rows, rows),
        check_vma=False,
    )
```

```python
import functools

import jax
import jax.numpy as jnp
from jax import lax
from jax.experimental import pallas as pl
from jax.experimental.pallas import tpu as pltpu
from jax.sharding import PartitionSpec as P

LANES = 128
SUBLANES = 8
SMALL = 8 << 20
PARTS = (2, 2, 4, 4, 4)
NN = (((1,), (0,)), ((), ()))
NT = (((1,), (1,)), ((), ()))
TN = (((0,), (0,)), ((), ()))


def matmul(a, b, dims):
    return lax.dot_general(a, b, dims, preferred_element_type=jnp.float32)


def slots(ids, experts):
    tokens = ids.shape[1]
    which = lax.broadcasted_iota(jnp.int32, (experts, tokens), 0)
    first, second = which == ids[0:1], which == ids[1:2]
    named = jnp.where(first | second, 1.0, 0.0).astype(jnp.bfloat16)
    before = lax.broadcasted_iota(jnp.int32, (tokens, tokens), 0) < lax.broadcasted_iota(
        jnp.int32, (tokens, tokens), 1
    )
    earlier = matmul(named, jnp.where(before, 1.0, 0.0).astype(jnp.bfloat16), NN)
    return [
        jnp.sum(jnp.where(mine, earlier, 0.0), axis=0, keepdims=True).astype(jnp.int32)
        for mine in (first, second)
    ]


def pick_rows(ids, slot, rows, per_peer, rest):
    shift = rest.bit_length() - 1
    half = lax.axis_index("half")
    row = lax.broadcasted_iota(jnp.int32, (rows, ids.shape[1]), 0)
    hits = []
    for k in range(2):
        e = ids[k : k + 1]
        peer = ((e >> (shift + 1)) << shift) | (e & (rest - 1))
        mine = ((e >> shift) & 1) == half
        hits.append(row == jnp.where(mine, peer * per_peer + slot[k], -1))
    return jnp.where(hits[0] | hits[1], 1.0, 0.0).astype(jnp.bfloat16)


def route_body(experts, per_peer, rest, ids_ref, tok_ref, send_ref, target_ref, late_ref):
    ids = ids_ref[...]
    slot = slots(ids, experts)
    for k in range(2):
        target_ref[k : k + 1, :] = ids[k : k + 1] * per_peer + slot[k]
    late_ref[...] = tok_ref[tok_ref.shape[0] - late_ref.shape[0] :, :]
    near_pick = pick_rows(ids, slot, send_ref.shape[0], per_peer, rest)
    send_ref[...] = matmul(near_pick, tok_ref[...], NN).astype(jnp.bfloat16)


def route(ids, tokens, early, experts, per_peer, rest):
    rows, width = experts // 2 * per_peer, tokens.shape[1]
    return pl.pallas_call(
        functools.partial(route_body, experts, per_peer, rest),
        out_shape=(
            jax.ShapeDtypeStruct((rows, width), jnp.bfloat16),
            jax.ShapeDtypeStruct(ids.shape, jnp.int32),
            jax.ShapeDtypeStruct((tokens.shape[0] - early, width), jnp.bfloat16),
        ),
        cost_estimate=pl.CostEstimate(
            flops=2 * rows * tokens.shape[0] * width,
            bytes_accessed=2 * (rows + tokens.shape[0]) * width,
            transcendentals=0,
        ),
        compiler_params=pltpu.CompilerParams(vmem_limit_bytes=60 << 20),
        name="route",
    )(ids, tokens)


def gather_first_body(
    experts, per_peer, rest, ids_ref, tok_ref, target_ref, gate_ref, part_ref, pick_ref, weight_ref
):
    row = lax.broadcasted_iota(jnp.int32, weight_ref.shape[::-1], 0)
    weight = jnp.where(row == target_ref[1:2, :], gate_ref[1:2, :], 0.0)
    weight = jnp.where(row == target_ref[0:1, :], gate_ref[0:1, :], weight)
    weight_ref[...] = weight.T.astype(jnp.bfloat16)
    ids = ids_ref[...]
    pick = pick_rows(ids, slots(ids, experts), part_ref.shape[0], per_peer, rest)
    count = tok_ref.shape[0]
    part_ref[...] = matmul(pick[:, :count], tok_ref[...], NN).astype(jnp.bfloat16)
    pick_ref[...] = pick[:, count:]


def gather_first(ids, tokens, target, gates, experts, per_peer, rest):
    rows, width = experts // 2 * per_peer, tokens.shape[1]
    return pl.pallas_call(
        functools.partial(gather_first_body, experts, per_peer, rest),
        out_shape=(
            jax.ShapeDtypeStruct((rows, width), jnp.bfloat16),
            jax.ShapeDtypeStruct((rows, ids.shape[1] - tokens.shape[0]), jnp.bfloat16),
            jax.ShapeDtypeStruct((ids.shape[1], experts * per_peer), jnp.bfloat16),
        ),
        compiler_params=pltpu.CompilerParams(vmem_limit_bytes=SMALL),
        cost_estimate=pl.CostEstimate(flops=40 * 10**9, bytes_accessed=0, transcendentals=0),
        name="gather_first",
    )(ids, tokens, target, gates)


def gather_last_body(pick_ref, tok_ref, part_ref, send_ref):
    rows = matmul(pick_ref[...], tok_ref[...], NN) + part_ref[...].astype(jnp.float32)
    send_ref[...] = rows.astype(jnp.bfloat16)


def gather_last(pick, tokens, part):
    rows, count = pick.shape
    return pl.pallas_call(
        gather_last_body,
        out_shape=jax.ShapeDtypeStruct(part.shape, jnp.bfloat16),
        compiler_params=pltpu.CompilerParams(vmem_limit_bytes=SMALL),
        cost_estimate=pl.CostEstimate(
            flops=2 * rows * count * part.shape[1], bytes_accessed=0, transcendentals=0
        ),
        name="gather_last",
    )(pick, tokens, part)


def expert_body(sizes, packed, far, *refs):
    x_hbm, p_hbm, wo_hbm, wi_hbm = refs[:4]
    near_hbm = refs[4] if far else None
    o_ref, x, acc, gsum, sem, *bufs = refs[4 + far :]
    rows, width = x.shape
    blocks = len(sizes)
    p, wo, wi = bufs[:blocks], bufs[blocks : 2 * blocks], bufs[2 * blocks :]
    own = lax.axis_index("half")
    half = 1 - own if far else own

    def block(j):
        return pl.ds(sum(sizes[:j]), sizes[j])

    def up(j):
        return pltpu.make_async_copy(wo_hbm.at[block(j), :], wo[j], sem.at[0, j])

    def pre(j):
        return pltpu.make_async_copy(p_hbm.at[:, half, :, block(j)], p[j], sem.at[1, j])

    def down(j):
        return pltpu.make_async_copy(wi_hbm.at[:, block(j)], wi[j], sem.at[2, j])

    rows_in = pltpu.make_async_copy(x_hbm, x, sem.at[3, 0])
    rows_in.start()
    for j in range(blocks):
        up(j).start()
        pre(j).start()
        down(j).start()
    if far:
        near = pltpu.make_async_copy(near_hbm, o_ref.at[:, own], sem.at[3, 1])
        near.start()
    rows_in.wait()
    up(0).wait()
    upstream = matmul(x[...], wo[0][...], NT)
    for j in range(blocks):
        pre(j).wait()
        down(j).wait()
        following = None
        if j + 1 < blocks:
            up(j + 1).wait()
            following = matmul(x[...], wo[j + 1][...], NT)
        act = p[j][...].astype(jnp.float32).reshape(rows, sizes[j])
        prod = jnp.maximum(act, 0.0) * upstream
        part = prod[:, :LANES]
        for q in range(1, sizes[j] // LANES):
            part = part + prod[:, q * LANES : (q + 1) * LANES]
        hidden = jnp.where(act > 0, upstream, 0.0).astype(jnp.bfloat16)
        back = matmul(hidden, wi[j][...], NT)
        if j == 0:
            acc[...] = back
            gsum[...] = part
        else:
            acc[...] += back
            gsum[...] += part
        upstream = following
    dots = jnp.sum(gsum[...], axis=1, keepdims=True)
    high = dots.astype(jnp.bfloat16).astype(jnp.float32)
    low = dots - high
    out = acc[...].astype(jnp.bfloat16)
    if far:
        near.wait()
    dst = o_ref.at[:, half] if far else o_ref
    if not packed:
        lane = lax.broadcasted_iota(jnp.int32, (rows, LANES), 1)
        tail = jnp.where(lane == 0, high, jnp.where(lane == 1, low, 0.0)).astype(jnp.bfloat16)
        dst[:, :, :width] = out.reshape(*dst.shape[:2], width)
        dst[:, :, width:] = tail.reshape(*dst.shape[:2], LANES)
        return
    outer, rest = dst.shape[:2]
    peers = outer * rest
    groups, cols = rows // peers // SUBLANES, width // LANES
    lane = lax.broadcasted_iota(jnp.int32, (peers, SUBLANES, LANES), 2)
    out = out.reshape(peers, groups, SUBLANES, width)
    high = high.reshape(peers, groups, SUBLANES, 1)
    low = low.reshape(peers, groups, SUBLANES, 1)
    tail = jnp.zeros((peers, SUBLANES, LANES), jnp.float32)
    for r in range(groups):
        tail = jnp.where(lane == 2 * r, high[:, r], tail)
        tail = jnp.where(lane == 2 * r + 1, low[:, r], tail)
        for c in range(cols):
            at = (r * cols + c) * SUBLANES
            dst[:, :, at : at + SUBLANES, :] = out[:, r, :, c * LANES : (c + 1) * LANES].reshape(
                outer, rest, SUBLANES, LANES
            )
    dst[:, :, groups * cols * SUBLANES :, :] = tail.astype(jnp.bfloat16).reshape(
        outer, rest, SUBLANES, LANES
    )


def expert(x, p, wo, wi, rest, near=None):
    rows, width = x.shape
    outer, _, group, hidden = p.shape
    sizes = [part * hidden // sum(PARTS) for part in PARTS]
    per_peer = group // rest
    far = near is not None
    packed = per_peer % SUBLANES == 0
    both = (2,) if far else ()
    shape = (
        (outer, *both, rest, per_peer * (width // LANES) + SUBLANES, LANES)
        if packed
        else (outer, *both, group, width + LANES)
    )
    operands = (x, p, wo, wi) + ((near,) if far else ())
    return pl.pallas_call(
        functools.partial(expert_body, sizes, packed, int(far)),
        out_shape=jax.ShapeDtypeStruct(shape, jnp.bfloat16),
        in_specs=[pl.BlockSpec(memory_space=pl.ANY)] * len(operands),
        out_specs=pl.BlockSpec(memory_space=pltpu.VMEM),
        scratch_shapes=[
            pltpu.VMEM((rows, width), jnp.bfloat16),
            pltpu.VMEM((rows, width), jnp.float32),
            pltpu.VMEM((rows, LANES), jnp.float32),
            pltpu.SemaphoreType.DMA((4, len(sizes))),
        ]
        + [pltpu.VMEM((outer, group, size), jnp.bfloat16) for size in sizes]
        + [pltpu.VMEM((size, width), jnp.bfloat16) for size in sizes]
        + [pltpu.VMEM((width, size), jnp.bfloat16) for size in sizes],
        compiler_params=pltpu.CompilerParams(vmem_limit_bytes=50 << 20),
        cost_estimate=pl.CostEstimate(
            flops=4 * rows * width * hidden,
            bytes_accessed=2 * (rows * hidden + 2 * width * hidden + 2 * rows * width),
            transcendentals=0,
        ),
        name="expert_far" if far else "expert_near",
    )(*operands)


def combine_body(packed, target_ref, weight_ref, back_ref, grad_ref, dots_ref):
    tokens, width = grad_ref.shape
    if packed:
        peers = back_ref.shape[0]
        cols = width // LANES
        groups = back_ref.shape[1] // SUBLANES // cols
        rows = peers * groups * SUBLANES
    else:
        rows = back_ref.shape[0]
    row = lax.broadcasted_iota(jnp.int32, (rows, tokens), 0)
    hit = [row == target_ref[k : k + 1, :] for k in range(2)]
    weight = weight_ref[...]
    if packed:

        def column(c):
            return jnp.stack(
                [
                    back_ref[:, (r * cols + c) * SUBLANES : (r * cols + c + 1) * SUBLANES, :]
                    for r in range(groups)
                ],
                axis=1,
            ).reshape(rows, LANES)

        tail = back_ref[:, groups * cols * SUBLANES :, :].astype(jnp.float32)
        lane = lax.broadcasted_iota(jnp.int32, tail.shape, 2)
        sums = (
            jnp.stack([jnp.where(lane // 2 == r, tail, 0.0) for r in range(groups)], axis=1)
            .reshape(rows, LANES)
            .astype(jnp.bfloat16)
        )
        for c in range(0, cols, 2):
            part = jnp.concatenate([column(c), column(c + 1)], axis=1)
            grad_ref[:, c * LANES : (c + 2) * LANES] = matmul(weight, part, NN).astype(
                jnp.bfloat16
            )
    else:
        part = back_ref[:, :width]
        grad_ref[...] = matmul(weight, part, NN).astype(jnp.bfloat16)
        sums = back_ref[:, width:]
    for k in range(2):
        pick = jnp.where(hit[k], 1.0, 0.0).astype(jnp.bfloat16)
        dots_ref[k : k + 1, :] = jnp.sum(matmul(sums, pick, TN), axis=0, keepdims=True)


def combine(target, weight, back, width):
    tokens = target.shape[1]
    packed = back.ndim == 3
    return pl.pallas_call(
        functools.partial(combine_body, packed),
        out_shape=(
            jax.ShapeDtypeStruct((tokens, width), jnp.bfloat16),
            jax.ShapeDtypeStruct(target.shape, jnp.float32),
        ),
        compiler_params=pltpu.CompilerParams(vmem_limit_bytes=16 << 20),
        name="combine",
    )(target, weight, back)


def per_device(output_grad, expert_ids, gate_weights, pre_act, w_in, w_out):
    outer, rest = lax.axis_size("outer"), lax.axis_size("rest")
    devices = 2 * outer * rest
    width = output_grad.shape[1]
    cap_rows, hidden = pre_act.shape[1:]
    per_peer = cap_rows // devices
    group = rest * per_peer
    swap = [(0, 1), (1, 0)]

    def exchange(x, axes):
        return lax.all_to_all(x, axes, split_axis=0, concat_axis=0, tiled=True)

    def to_half(rows):
        peers = rows.reshape(outer * rest, per_peer, width)
        return exchange(peers, ("outer", "rest")).reshape(outer * group, width)

    ids = expert_ids.T
    far_ids = lax.ppermute(ids, "half", swap)
    early = output_grad.shape[0] * 15 // 32
    first = lax.ppermute(output_grad[:early], "half", swap)
    send, target, late = route(ids, output_grad, early, devices, per_peer, rest)
    second = lax.ppermute(late, "half", swap)
    near_rows = to_half(send)
    gates = gate_weights.T
    part, pick, weight = gather_first(far_ids, first, target, gates, devices, per_peer, rest)
    far_rows = to_half(gather_last(pick, second, part))
    act = pre_act.reshape(outer, 2, group, hidden)
    near = expert(near_rows, act, w_out[0], w_in[0], rest)
    result = expert(far_rows, act, w_out[0], w_in[0], rest, near)
    if result.ndim == 5:
        result = result.reshape(devices, *result.shape[3:])
    else:
        result = result.reshape(devices, per_peer, -1)
    back = exchange(result, ("outer", "half", "rest"))
    if per_peer % SUBLANES:
        back = back.reshape(cap_rows, -1)
    input_grad, gate_grad = combine(target, weight, back, width)
    return input_grad, gate_grad.T


def solution(mesh):
    outer, inner = mesh.shape["outer"], mesh.shape["inner"]
    split = jax.sharding.Mesh(
        mesh.devices.reshape(outer, 2, inner // 2), ("outer", "half", "rest")
    )
    axes = ("outer", "half", "rest")
    rows, blocks = P(axes, None), P(axes, None, None)
    return jax.shard_map(
        per_device,
        mesh=split,
        in_specs=(rows, rows, rows, blocks, blocks, blocks),
        out_specs=(rows, rows),
        check_vma=False,
    )
```

```python
import functools

import jax
import jax.numpy as jnp
from jax import lax
from jax.experimental import pallas as pl
from jax.experimental.pallas import tpu as pltpu
from jax.sharding import PartitionSpec as P

LANES = 128
SUBLANES = 8
SMALL = 8 << 20
PARTS = (2, 2, 4, 4, 4)
NN = (((1,), (0,)), ((), ()))
NT = (((1,), (1,)), ((), ()))
TN = (((0,), (0,)), ((), ()))


def matmul(a, b, dims):
    return lax.dot_general(a, b, dims, preferred_element_type=jnp.float32)


def slots(ids, experts):
    tokens = ids.shape[1]
    which = lax.broadcasted_iota(jnp.int32, (experts, tokens), 0)
    first, second = which == ids[0:1], which == ids[1:2]
    named = jnp.where(first | second, 1.0, 0.0).astype(jnp.bfloat16)
    before = lax.broadcasted_iota(jnp.int32, (tokens, tokens), 0) < lax.broadcasted_iota(
        jnp.int32, (tokens, tokens), 1
    )
    earlier = matmul(named, jnp.where(before, 1.0, 0.0).astype(jnp.bfloat16), NN)
    return [
        jnp.sum(jnp.where(mine, earlier, 0.0), axis=0, keepdims=True).astype(jnp.int32)
        for mine in (first, second)
    ]


def pick_rows(ids, slot, rows, per_peer, rest):
    shift = rest.bit_length() - 1
    half = lax.axis_index("half")
    row = lax.broadcasted_iota(jnp.int32, (rows, ids.shape[1]), 0)
    hits = []
    for k in range(2):
        e = ids[k : k + 1]
        peer = ((e >> (shift + 1)) << shift) | (e & (rest - 1))
        mine = ((e >> shift) & 1) == half
        hits.append(row == jnp.where(mine, peer * per_peer + slot[k], -1))
    return jnp.where(hits[0] | hits[1], 1.0, 0.0).astype(jnp.bfloat16)


def route_body(experts, per_peer, rest, ids_ref, tok_ref, send_ref, target_ref, late_ref):
    ids = ids_ref[...]
    slot = slots(ids, experts)
    for k in range(2):
        target_ref[k : k + 1, :] = ids[k : k + 1] * per_peer + slot[k]
    late_ref[...] = tok_ref[tok_ref.shape[0] - late_ref.shape[0] :, :]
    near_pick = pick_rows(ids, slot, send_ref.shape[0], per_peer, rest)
    send_ref[...] = matmul(near_pick, tok_ref[...], NN).astype(jnp.bfloat16)


def route(ids, tokens, early, experts, per_peer, rest):
    rows, width = experts // 2 * per_peer, tokens.shape[1]
    return pl.pallas_call(
        functools.partial(route_body, experts, per_peer, rest),
        out_shape=(
            jax.ShapeDtypeStruct((rows, width), jnp.bfloat16),
            jax.ShapeDtypeStruct(ids.shape, jnp.int32),
            jax.ShapeDtypeStruct((tokens.shape[0] - early, width), jnp.bfloat16),
        ),
        cost_estimate=pl.CostEstimate(
            flops=2 * rows * tokens.shape[0] * width,
            bytes_accessed=2 * (rows + tokens.shape[0]) * width,
            transcendentals=0,
        ),
        compiler_params=pltpu.CompilerParams(vmem_limit_bytes=60 << 20),
        name="route",
    )(ids, tokens)


def gather_first_body(
    experts, per_peer, rest, ids_ref, tok_ref, target_ref, gate_ref, part_ref, pick_ref, weight_ref
):
    row = lax.broadcasted_iota(jnp.int32, weight_ref.shape[::-1], 0)
    weight = jnp.where(row == target_ref[1:2, :], gate_ref[1:2, :], 0.0)
    weight = jnp.where(row == target_ref[0:1, :], gate_ref[0:1, :], weight)
    weight_ref[...] = weight.T.astype(jnp.bfloat16)
    ids = ids_ref[...]
    pick = pick_rows(ids, slots(ids, experts), part_ref.shape[0], per_peer, rest)
    count = tok_ref.shape[0]
    part_ref[...] = matmul(pick[:, :count], tok_ref[...], NN).astype(jnp.bfloat16)
    pick_ref[...] = pick[:, count:]


def gather_first(ids, tokens, target, gates, experts, per_peer, rest):
    rows, width = experts // 2 * per_peer, tokens.shape[1]
    return pl.pallas_call(
        functools.partial(gather_first_body, experts, per_peer, rest),
        out_shape=(
            jax.ShapeDtypeStruct((rows, width), jnp.bfloat16),
            jax.ShapeDtypeStruct((rows, ids.shape[1] - tokens.shape[0]), jnp.bfloat16),
            jax.ShapeDtypeStruct((ids.shape[1], experts * per_peer), jnp.bfloat16),
        ),
        compiler_params=pltpu.CompilerParams(vmem_limit_bytes=SMALL),
        cost_estimate=pl.CostEstimate(flops=40 * 10**9, bytes_accessed=0, transcendentals=0),
        name="gather_first",
    )(ids, tokens, target, gates)


def gather_last_body(pick_ref, tok_ref, part_ref, send_ref):
    rows = matmul(pick_ref[...], tok_ref[...], NN) + part_ref[...].astype(jnp.float32)
    send_ref[...] = rows.astype(jnp.bfloat16)


def gather_last(pick, tokens, part):
    rows, count = pick.shape
    return pl.pallas_call(
        gather_last_body,
        out_shape=jax.ShapeDtypeStruct(part.shape, jnp.bfloat16),
        compiler_params=pltpu.CompilerParams(vmem_limit_bytes=SMALL),
        cost_estimate=pl.CostEstimate(
            flops=2 * rows * count * part.shape[1], bytes_accessed=0, transcendentals=0
        ),
        name="gather_last",
    )(pick, tokens, part)


def expert_body(sizes, packed, far, *refs):
    x_hbm, p_hbm, wo_hbm, wi_hbm = refs[:4]
    near_hbm = refs[4] if far else None
    o_ref, x, acc, gsum, sem, *bufs = refs[4 + far :]
    rows, width = x.shape
    blocks = len(sizes)
    p, wo, wi = bufs[:blocks], bufs[blocks : 2 * blocks], bufs[2 * blocks :]
    own = lax.axis_index("half")
    half = 1 - own if far else own

    def block(j):
        return pl.ds(sum(sizes[:j]), sizes[j])

    def up(j):
        return pltpu.make_async_copy(wo_hbm.at[block(j), :], wo[j], sem.at[0, j])

    def pre(j):
        return pltpu.make_async_copy(p_hbm.at[:, half, :, block(j)], p[j], sem.at[1, j])

    def down(j):
        return pltpu.make_async_copy(wi_hbm.at[:, block(j)], wi[j], sem.at[2, j])

    rows_in = pltpu.make_async_copy(x_hbm, x, sem.at[3, 0])
    rows_in.start()
    for j in range(blocks):
        up(j).start()
        pre(j).start()
        down(j).start()
    if far:
        near = pltpu.make_async_copy(near_hbm, o_ref.at[:, own], sem.at[3, 1])
        near.start()
    rows_in.wait()
    up(0).wait()
    upstream = matmul(x[...], wo[0][...], NT)
    for j in range(blocks):
        pre(j).wait()
        down(j).wait()
        following = None
        if j + 1 < blocks:
            up(j + 1).wait()
            following = matmul(x[...], wo[j + 1][...], NT)
        act = p[j][...].astype(jnp.float32).reshape(rows, sizes[j])
        prod = jnp.maximum(act, 0.0) * upstream
        part = prod[:, :LANES]
        for q in range(1, sizes[j] // LANES):
            part = part + prod[:, q * LANES : (q + 1) * LANES]
        hidden = jnp.where(act > 0, upstream, 0.0).astype(jnp.bfloat16)
        back = matmul(hidden, wi[j][...], NT)
        if j == 0:
            acc[...] = back
            gsum[...] = part
        else:
            acc[...] += back
            gsum[...] += part
        upstream = following
    dots = jnp.sum(gsum[...], axis=1, keepdims=True)
    high = dots.astype(jnp.bfloat16).astype(jnp.float32)
    low = dots - high
    out = acc[...].astype(jnp.bfloat16)
    if far:
        near.wait()
    dst = o_ref.at[:, half] if far else o_ref
    if not packed:
        lane = lax.broadcasted_iota(jnp.int32, (rows, LANES), 1)
        tail = jnp.where(lane == 0, high, jnp.where(lane == 1, low, 0.0)).astype(jnp.bfloat16)
        dst[:, :, :width] = out.reshape(*dst.shape[:2], width)
        dst[:, :, width:] = tail.reshape(*dst.shape[:2], LANES)
        return
    outer, rest = dst.shape[:2]
    peers = outer * rest
    groups, cols = rows // peers // SUBLANES, width // LANES
    lane = lax.broadcasted_iota(jnp.int32, (peers, SUBLANES, LANES), 2)
    out = out.reshape(peers, groups, SUBLANES, width)
    high = high.reshape(peers, groups, SUBLANES, 1)
    low = low.reshape(peers, groups, SUBLANES, 1)
    tail = jnp.zeros((peers, SUBLANES, LANES), jnp.float32)
    for r in range(groups):
        tail = jnp.where(lane == 2 * r, high[:, r], tail)
        tail = jnp.where(lane == 2 * r + 1, low[:, r], tail)
        for c in range(cols):
            at = (r * cols + c) * SUBLANES
            dst[:, :, at : at + SUBLANES, :] = out[:, r, :, c * LANES : (c + 1) * LANES].reshape(
                outer, rest, SUBLANES, LANES
            )
    dst[:, :, groups * cols * SUBLANES :, :] = tail.astype(jnp.bfloat16).reshape(
        outer, rest, SUBLANES, LANES
    )


def expert(x, p, wo, wi, rest, near=None):
    rows, width = x.shape
    outer, _, group, hidden = p.shape
    sizes = [part * hidden // sum(PARTS) for part in PARTS]
    per_peer = group // rest
    far = near is not None
    packed = per_peer % SUBLANES == 0
    both = (2,) if far else ()
    shape = (
        (outer, *both, rest, per_peer * (width // LANES) + SUBLANES, LANES)
        if packed
        else (outer, *both, group, width + LANES)
    )
    operands = (x, p, wo, wi) + ((near,) if far else ())
    return pl.pallas_call(
        functools.partial(expert_body, sizes, packed, int(far)),
        out_shape=jax.ShapeDtypeStruct(shape, jnp.bfloat16),
        in_specs=[pl.BlockSpec(memory_space=pl.ANY)] * len(operands),
        out_specs=pl.BlockSpec(memory_space=pltpu.VMEM),
        scratch_shapes=[
            pltpu.VMEM((rows, width), jnp.bfloat16),
            pltpu.VMEM((rows, width), jnp.float32),
            pltpu.VMEM((rows, LANES), jnp.float32),
            pltpu.SemaphoreType.DMA((4, len(sizes))),
        ]
        + [pltpu.VMEM((outer, group, size), jnp.bfloat16) for size in sizes]
        + [pltpu.VMEM((size, width), jnp.bfloat16) for size in sizes]
        + [pltpu.VMEM((width, size), jnp.bfloat16) for size in sizes],
        compiler_params=pltpu.CompilerParams(vmem_limit_bytes=50 << 20),
        cost_estimate=pl.CostEstimate(
            flops=4 * rows * width * hidden,
            bytes_accessed=2 * (rows * hidden + 2 * width * hidden + 2 * rows * width),
            transcendentals=0,
        ),
        name="expert_far" if far else "expert_near",
    )(*operands)


def combine_body(packed, target_ref, weight_ref, back_ref, grad_ref, dots_ref):
    tokens, width = grad_ref.shape
    if packed:
        peers = back_ref.shape[0]
        cols = width // LANES
        groups = back_ref.shape[1] // SUBLANES // cols
        rows = peers * groups * SUBLANES
    else:
        rows = back_ref.shape[0]
    row = lax.broadcasted_iota(jnp.int32, (rows, tokens), 0)
    hit = [row == target_ref[k : k + 1, :] for k in range(2)]
    weight = weight_ref[...]
    if packed:

        def column(c):
            return jnp.stack(
                [
                    back_ref[:, (r * cols + c) * SUBLANES : (r * cols + c + 1) * SUBLANES, :]
                    for r in range(groups)
                ],
                axis=1,
            ).reshape(rows, LANES)

        tail = back_ref[:, groups * cols * SUBLANES :, :].astype(jnp.float32)
        lane = lax.broadcasted_iota(jnp.int32, tail.shape, 2)
        sums = (
            jnp.stack([jnp.where(lane // 2 == r, tail, 0.0) for r in range(groups)], axis=1)
            .reshape(rows, LANES)
            .astype(jnp.bfloat16)
        )
        part = jnp.concatenate([column(c) for c in range(cols)], axis=1)
        grad_ref[...] = matmul(weight, part, NN).astype(jnp.bfloat16)
    else:
        part = back_ref[:, :width]
        grad_ref[...] = matmul(weight, part, NN).astype(jnp.bfloat16)
        sums = back_ref[:, width:]
    for k in range(2):
        pick = jnp.where(hit[k], 1.0, 0.0).astype(jnp.bfloat16)
        dots_ref[k : k + 1, :] = jnp.sum(matmul(sums, pick, TN), axis=0, keepdims=True)


def combine(target, weight, back, width):
    tokens = target.shape[1]
    packed = back.ndim == 3
    return pl.pallas_call(
        functools.partial(combine_body, packed),
        out_shape=(
            jax.ShapeDtypeStruct((tokens, width), jnp.bfloat16),
            jax.ShapeDtypeStruct(target.shape, jnp.float32),
        ),
        compiler_params=pltpu.CompilerParams(vmem_limit_bytes=16 << 20),
        name="combine",
    )(target, weight, back)


def per_device(output_grad, expert_ids, gate_weights, pre_act, w_in, w_out):
    outer, rest = lax.axis_size("outer"), lax.axis_size("rest")
    devices = 2 * outer * rest
    width = output_grad.shape[1]
    cap_rows, hidden = pre_act.shape[1:]
    per_peer = cap_rows // devices
    group = rest * per_peer
    swap = [(0, 1), (1, 0)]

    def exchange(x, axes):
        return lax.all_to_all(x, axes, split_axis=0, concat_axis=0, tiled=True)

    def to_half(rows):
        peers = rows.reshape(outer * rest, per_peer, width)
        return exchange(peers, ("outer", "rest")).reshape(outer * group, width)

    ids = expert_ids.T
    far_ids = lax.ppermute(ids, "half", swap)
    early = output_grad.shape[0] * 15 // 32
    first = lax.ppermute(output_grad[:early], "half", swap)
    send, target, late = route(ids, output_grad, early, devices, per_peer, rest)
    second = lax.ppermute(late, "half", swap)
    near_rows = to_half(send)
    gates = gate_weights.T
    part, pick, weight = gather_first(far_ids, first, target, gates, devices, per_peer, rest)
    far_rows = to_half(gather_last(pick, second, part))
    act = pre_act.reshape(outer, 2, group, hidden)
    near = expert(near_rows, act, w_out[0], w_in[0], rest)
    result = expert(far_rows, act, w_out[0], w_in[0], rest, near)
    if result.ndim == 5:
        result = result.reshape(devices, *result.shape[3:])
    else:
        result = result.reshape(devices, per_peer, -1)
    back = exchange(result, ("outer", "half", "rest"))
    if per_peer % SUBLANES:
        back = back.reshape(cap_rows, -1)
    input_grad, gate_grad = combine(target, weight, back, width)
    return input_grad, gate_grad.T


def solution(mesh):
    outer, inner = mesh.shape["outer"], mesh.shape["inner"]
    split = jax.sharding.Mesh(
        mesh.devices.reshape(outer, 2, inner // 2), ("outer", "half", "rest")
    )
    axes = ("outer", "half", "rest")
    rows, blocks = P(axes, None), P(axes, None, None)
    return jax.shard_map(
        per_device,
        mesh=split,
        in_specs=(rows, rows, rows, blocks, blocks, blocks),
        out_specs=(rows, rows),
        check_vma=False,
    )
```
